256 devices in a mesh: ta: 4 (over x), sa: 64 (over y, z, core).
Axes of the slice: x: 4, y: 4, z: 8, core: 2. Of those that a mesh axis runs over, the one named last changes fastest.
Arguments:
- snapshots: float32 [256, 2, 262144], P('ta', None, 'sa'), may hold values from -6 to 6
- bins: int32 [16], replicated, may hold values from 0 to 127, as said below
- eigenvalues: float32 [16, 32], P('ta'), may hold values from 100 to 1000
- old_basis: bfloat16 [16, 2, 32, 2, 262144], P('ta', None, None, None, 'sa'), may hold values from -0.0055242717 to 0.0055242717, as said below
- block_count: int32 [1], replicated, may hold values from 1 to 8
Outputs:
- new_basis: bfloat16 [16, 2, 32, 2, 262144], P('ta', None, None, None, 'sa')
- coherence: float32 [16, 2, 32, 32], P('ta')
The draws below stay inside these ranges and needn't reach their ends.
Inputs may be any that keep to these rules, and one draw needn't show every extreme that they name: The 16 bins are distinct; 0 and 127 are always among them. `old_basis`: every entry lies within 4 / sqrt(524288) in magnitude.
All inputs are finite; a program needn't handle non-finite values.
Results may differ from the reference program's by a relative error of at most 0.001.
Values sent between devices are 32-bit elements; how exact they have to be, the bound alone decides.
No kernel may reach another device: no remote copies, remote signals or barrier semaphores. Data moves between devices by JAX's collectives and lax.ppermute only.
A program may use at most 128 MiB of HBM per device.

```python
import math
import jax
import jax.numpy as jnp
from jax import lax

NT = 256
NBINS = 16
RANK = 32
NS = 262144


def draw_bins(key, part):
    half = NT // 2
    inner = jax.random.permutation(key, half - 2)[:NBINS - 2].astype(jnp.int32) + 1
    full = jnp.concatenate([jnp.array([0, half - 1], jnp.int32), inner])
    order = jax.random.permutation(jax.random.fold_in(key, 7), NBINS)
    return full[order]


def draw_old_basis(key, part):
    own_key = jax.random.fold_in(key, 11)
    common_key = jax.random.fold_in(key, 12)
    angle_key = jax.random.fold_in(key, 13)
    shape = (NBINS, 2, RANK, 2, NS)
    common_shape = (NBINS, 2, 2, NS)
    own = jnp.clip(jax.random.normal(own_key, shape, jnp.float32), -4.0, 4.0)
    common = jnp.clip(jax.random.normal(common_key, common_shape, jnp.float32), -4.0, 4.0)
    share = 0.5
    theta = jax.random.uniform(angle_key, (NBINS, RANK), jnp.float32, -math.pi, math.pi)
    cosine = jnp.cos(theta)[:, :, None, None]
    sine = jnp.sin(theta)[:, :, None, None]
    common_re = common[:, 0][:, None, :, :]
    common_im = common[:, 1][:, None, :, :]
    rotated_re = common_re * cosine - common_im * sine
    rotated_im = common_re * sine + common_im * cosine
    rotated = jnp.stack([rotated_re, rotated_im], axis=1)
    limit = 4.0 * (1.0 - 2.0 ** (-8))
    mixed = jnp.clip(own + share * rotated, -limit, limit)
    return (mixed * (2.0 * NS) ** (-0.5)).astype(jnp.bfloat16)


def block_levels(key, shape, cuts, smallest, high):
    loudness = 1.0
    for axis_at, parts in cuts:
        steps = jax.random.uniform(jax.random.fold_in(jax.random.fold_in(key, 6), axis_at), (parts,), jnp.float32, smallest / len(cuts), high / len(cuts))
        loudness = loudness * jnp.repeat(jnp.exp(steps), shape[axis_at] // parts).reshape((-1,) + (1,) * (len(shape) - 1 - axis_at))
    return loudness


def gaussian(key, dims, scale, most, split=(), kind=jnp.bfloat16):
    level = block_levels(key, dims, split, -0.22, 0.18) if split else 1.0
    values = jax.random.normal(key, dims, jnp.float32) * scale * level
    return jnp.minimum(jnp.maximum(values, -most), most).astype(kind)


def setup_inputs(seed: int = 0) -> dict:
    splits = jax.random.split(jax.random.key(seed), 6)
    snapshots = gaussian(splits[0], (NT, 2, NS), 1.0, 6.0, ((0, 4), (2, 64)), jnp.float32)
    bins = draw_bins(jax.random.fold_in(splits[5], 71), 0)
    eigenvalues = jnp.clip(jnp.exp(math.log(1000.0) - 2.3025851 * jax.random.uniform(splits[2], (NBINS, RANK), jnp.float32) ** block_levels(splits[2], (NBINS, RANK), ((0, 4),), -0.2, 0.2)), 100.0, 1000.0)
    old_basis = draw_old_basis(jax.random.fold_in(splits[5], 71), 0)
    block_count = jax.random.randint(splits[4], (1,), 1, 9).astype(jnp.int32)
    return {"snapshots": snapshots, "bins": bins, "eigenvalues": eigenvalues, "old_basis": old_basis, "block_count": block_count}


def tables(bins, times, total):
    phase = bins[:, None] * times[None, :] % total
    angle = 2.0 * math.pi / total * phase.astype(jnp.float32)
    window = 0.5 - 0.5 * jnp.cos(2.0 * math.pi / total * times.astype(jnp.float32))
    scale = math.sqrt(8.0 / (3.0 * total))
    return (jnp.cos(angle) * window[None, :] * scale, -jnp.sin(angle) * window[None, :] * scale)

def update_bin(basis, spec, lam, w_old, w_new):
    hi = lax.Precision.HIGHEST
    u_re = basis[0].astype(jnp.float32)
    u_im = basis[1].astype(jnp.float32)
    s_re = spec[0]
    s_im = spec[1]
    c_re = jnp.dot(u_re, s_re, precision=hi) + jnp.dot(u_im, s_im, precision=hi)
    c_im = jnp.dot(u_re, s_im, precision=hi) - jnp.dot(u_im, s_re, precision=hi)
    scaled = w_old * lam
    g_re = scaled[:, None] * u_re + w_new * (c_re[:, None] * s_re[None, :] + c_im[:, None] * s_im[None, :])
    g_im = scaled[:, None] * u_im + w_new * (c_re[:, None] * s_im[None, :] - c_im[:, None] * s_re[None, :])
    gram_re = jnp.dot(g_re, g_re.T, precision=hi) + jnp.dot(g_im, g_im.T, precision=hi)
    gram_im = jnp.dot(g_re, g_im.T, precision=hi) - jnp.dot(g_im, g_re.T, precision=hi)
    inv = 1.0 / jnp.sqrt(jnp.diagonal(gram_re) + 1e-06)
    fresh = jnp.stack([g_re * inv[:, None], g_im * inv[:, None]]).astype(jnp.bfloat16)
    outer = inv[:, None] * inv[None, :]
    return (fresh, jnp.stack([gram_re * outer, gram_im * outer]))

def reference(snapshots, bins, eigenvalues, old_basis, block_count):
    total = snapshots.shape[0]
    points = snapshots.shape[2]
    times = jnp.arange(total, dtype=jnp.int32)
    c_tab, s_tab = tables(bins, times, total)
    flat = snapshots.reshape(total, 2 * points)
    hi = lax.Precision.HIGHEST
    spec = jnp.stack([jnp.dot(c_tab, flat, precision=hi), jnp.dot(s_tab, flat, precision=hi)], axis=1)
    count = block_count[0].astype(jnp.float32)
    w_old = count / (count + 1.0)
    w_new = 1.0 / (count + 1.0)
    basis = old_basis.reshape(old_basis.shape[0], 2, old_basis.shape[2], 2 * points)

    def one(items):
        return update_bin(items[0], items[1], items[2], w_old, w_new)
    fresh, coherence = lax.map(one, (basis, spec, eigenvalues))
    return (fresh.reshape(old_basis.shape), coherence)
```

```python
import math

import jax
import jax.numpy as jnp
from jax import lax
from jax.experimental import pallas as pl
from jax.experimental.pallas import tpu as pltpu
from jax.sharding import Mesh, PartitionSpec as P

SPACE = ("y", "z", "core")
HI = lax.Precision.HIGHEST
LANES = 128


def fold(v, axis):
    shape = v.shape
    lead, tiles = shape[:-2], shape[-1] // LANES
    v = v.reshape(*lead, 2, tiles, LANES)
    return jnp.swapaxes(v, axis, axis + 1).reshape(*lead, 2 * tiles, LANES)


def unfold(v, axis):
    lead, rows = v.shape[:-2], v.shape[-2]
    v = v.reshape(*lead, rows // 2, 2, LANES)
    return jnp.swapaxes(v, axis, axis + 1).reshape(*lead, 2, rows // 2 * LANES)


def transform_kernel(total, slice_len, rows, bins_ref, place_ref, x_ref, out_ref):
    n = 2 * bins_ref.shape[0]
    row = lax.broadcasted_iota(jnp.int32, (n, slice_len), 0)
    t = lax.broadcasted_iota(jnp.int32, (n, slice_len), 1) + place_ref[0] * slice_len
    which = jnp.zeros((n, slice_len), jnp.int32)
    for b in range(n // 2):
        which = jnp.where(row // 2 == b, bins_ref[b], which)
    phase = (which * t + (row % 2) * (total // 4)) % total
    step = 2.0 * math.pi / total
    window = 0.5 - 0.5 * jnp.cos(step * t.astype(jnp.float32))
    table = jnp.cos(step * phase.astype(jnp.float32)) * window * math.sqrt(8.0 / (3.0 * total))
    t_hi = table.astype(jnp.bfloat16)
    t_lo = (table - t_hi.astype(jnp.float32)).astype(jnp.bfloat16)
    left = jnp.concatenate([t_hi, t_lo], axis=0)
    left = jnp.concatenate([left, left], axis=1)
    for r in range(0, rows, 2):
        x = jnp.concatenate(
            [x_ref[pl.ds(r, slice_len, stride=rows), :], x_ref[pl.ds(r + 1, slice_len, stride=rows), :]],
            axis=1,
        )
        hi = x.astype(jnp.bfloat16)
        lo = (x - hi.astype(jnp.float32)).astype(jnp.bfloat16)
        res = jnp.dot(left, jnp.concatenate([hi, lo], axis=0), preferred_element_type=jnp.float32)
        res = res[:n] + res[n:]
        out_ref[pl.ds(r, n, stride=rows), :] = res[:, :LANES]
        out_ref[pl.ds(r + 1, n, stride=rows), :] = res[:, LANES:]


def project_kernel(nb, rank, parts_ref, u_ref, h_ref, s_ref, blk_ref, acc_ref):
    b = pl.program_id(0)
    rows = u_ref.shape[-2]

    @pl.when(b == 0)
    def _():
        acc_ref[...] = jnp.zeros_like(acc_ref)

    s = parts_ref[0, 0]
    for k in range(1, parts_ref.shape[0]):
        s = s + parts_ref[k, 0]
    s_ref[0] = s
    s_re, s_im = s[0], s[1]

    def eight(v):
        return v.reshape(rows // 8, 8, LANES).sum(axis=0)

    acc_ref[pl.ds((2 * nb * rank + b) * 8, 8), :] = eight(s_re * s_re + s_im * s_im)

    def body(j, carry):
        u_re = u_ref[0, 0, j].astype(jnp.float32)
        u_im = u_ref[0, 1, j].astype(jnp.float32)
        at = (b * 2 * rank + j) * 8
        acc_ref[pl.ds(pl.multiple_of(at, 8), 8), :] = eight(u_re * s_re + u_im * s_im)
        acc_ref[pl.ds(pl.multiple_of(at + rank * 8, 8), 8), :] = eight(u_re * s_im - u_im * s_re)
        return carry

    lax.fori_loop(0, rank, body, 0, unroll=4)

    @pl.when(b == nb - 1)
    def _():
        n = acc_ref.shape[0] // 8
        x = acc_ref[pl.ds(0, n, stride=8), :]
        for k in range(1, 8):
            x = x + acc_ref[pl.ds(k, n, stride=8), :]
        sums = lax.dot_general(
            jnp.ones((8, LANES), jnp.float32), x, (((1,), (1,)), ((), ())),
            precision=HI, preferred_element_type=jnp.float32,
        )
        blk = jnp.concatenate(
            [sums[0:1, k * LANES:(k + 1) * LANES] for k in range(3)] + [h_ref[...]], axis=0
        )
        blk_ref[...] = jnp.broadcast_to(blk[None], blk_ref.shape)


def update_kernel(nb, rank, count_ref, g_ref, eig_ref, s_ref, u_ref, out_ref, coh_ref, coef_ref):
    b, half = pl.program_id(0), pl.program_id(1)
    rows = u_ref.shape[-2]
    n_from = g_ref.shape[0] // 4

    @pl.when((b == 0) & (half == 0))
    def _():
        count = jnp.full((1, 1), count_ref[0], jnp.int32).astype(jnp.float32)
        w_old = count / (count + 1.0)
        w_new = 1.0 / (count + 1.0)
        sums = [g_ref[pl.ds(k, n_from, stride=4), :].sum(axis=0, keepdims=True) for k in range(3)]
        h = g_ref[pl.ds(3, n_from, stride=4), :]
        eye = lax.broadcasted_iota(jnp.int32, (rank, rank), 0) == lax.broadcasted_iota(jnp.int32, (rank, rank), 1)

        def col(v):
            return jnp.where(eye, v, 0.0).sum(axis=1, keepdims=True)

        for i in range(nb):
            at = (i % 2) * 2 * rank
            cr = sums[i // 2][:, at:at + rank]
            ci = sums[i // 2][:, at + rank:at + 2 * rank]
            power = sums[2][:, i:i + 1]
            a = w_old * eig_ref[i:i + 1, :]
            cr_c, ci_c, a_c = col(cr), col(ci), col(a)
            h_re = h[:rank, i * rank:(i + 1) * rank]
            h_im = h[rank:2 * rank, i * rank:(i + 1) * rank]
            both = w_new * (a_c + a + w_new * power)
            gram_re = a_c * a * h_re + (cr_c * cr + ci_c * ci) * both
            gram_im = a_c * a * h_im + (ci_c * cr - cr_c * ci) * both
            diag = jnp.where(eye, gram_re, 0.0)
            inv_c = 1.0 / jnp.sqrt(diag.sum(axis=1, keepdims=True) + 1e-06)
            inv_r = 1.0 / jnp.sqrt(diag.sum(axis=0, keepdims=True) + 1e-06)
            coh_ref[i, 0] = gram_re * inv_c * inv_r
            coh_ref[i, 1] = gram_im * inv_c * inv_r
            for k, v in enumerate((a_c * inv_c, w_new * cr_c * inv_c, w_new * ci_c * inv_c)):
                coef_ref[pl.ds((k * nb + i) * rank, rank), :] = jnp.broadcast_to(v, (rank, LANES))

    s_re, s_im = s_ref[0, 0], s_ref[0, 1]
    block = u_ref.shape[2]

    def body(j, carry):
        at = b * rank + half * block + j

        def coef(k):
            one = coef_ref[pl.ds(k * nb * rank + at, 1), :]
            return jnp.broadcast_to(one, (rows, LANES))

        alpha, beta, gamma = coef(0), coef(1), coef(2)
        u_re = u_ref[0, 0, j].astype(jnp.float32)
        u_im = u_ref[0, 1, j].astype(jnp.float32)
        out_ref[0, 0, j] = (alpha * u_re + (beta * s_re + gamma * s_im)).astype(out_ref.dtype)
        out_ref[0, 1, j] = (alpha * u_im + (beta * s_im - gamma * s_re)).astype(out_ref.dtype)
        return carry

    lax.fori_loop(0, block, body, 0, unroll=4)


def local(snapshots, bins, eigenvalues, old_basis, block_count):
    slice_len, _, points = snapshots.shape
    groups = lax.axis_size("ta")
    total = slice_len * groups
    rows = 2 * points // LANES
    nb, _, rank = old_basis.shape[:3]
    n_space = lax.axis_size(SPACE)
    place = lax.axis_index("ta").astype(jnp.int32).reshape(1)
    smem = pl.BlockSpec(memory_space=pltpu.SMEM)
    vmem = pl.BlockSpec(memory_space=pltpu.VMEM)

    x = fold(snapshots, 1).reshape(slice_len * rows, LANES)
    n = 2 * bins.shape[0]
    terms = pl.pallas_call(
        lambda *refs: transform_kernel(total, slice_len, rows, *refs),
        out_shape=jax.ShapeDtypeStruct((n * rows, LANES), jnp.float32),
        in_specs=[smem, smem, vmem],
        out_specs=vmem,
        name="transform",
    )(bins, place, x)
    parts = lax.all_to_all(terms.reshape(groups, n // groups * rows, LANES), "ta", 0, 0, tiled=True)
    parts = parts.reshape(groups, nb, 2, rows, LANES)

    u = fold(old_basis, 3)
    v = old_basis.reshape(nb, 2 * rank, 2 * points)
    vv = jnp.einsum("bjm,bkm->bjk", v, v, preferred_element_type=jnp.float32)
    h_re = vv[:, :rank, :rank] + vv[:, rank:, rank:]
    h_im = vv[:, :rank, rank:] - vv[:, rank:, :rank]
    h = jnp.concatenate([h_re, h_im], axis=1).transpose(1, 0, 2).reshape(2 * rank, 1, nb * rank)
    h = lax.all_to_all(h, SPACE, 0, 0, tiled=True).sum(axis=0)

    spec, blk = pl.pallas_call(
        lambda *refs: project_kernel(nb, rank, *refs),
        grid=(nb,),
        out_shape=(
            jax.ShapeDtypeStruct((nb, 2, rows, LANES), jnp.float32),
            jax.ShapeDtypeStruct((n_space, 4, LANES), jnp.float32),
        ),
        in_specs=[
            pl.BlockSpec((groups, 1, 2, rows, LANES), lambda b: (0, b, 0, 0, 0)),
            pl.BlockSpec((1, 2, rank, rows, LANES), lambda b: (b, 0, 0, 0, 0)),
            pl.BlockSpec((1, LANES), lambda b: (0, 0)),
        ],
        out_specs=(
            pl.BlockSpec((1, 2, rows, LANES), lambda b: (b, 0, 0, 0)),
            pl.BlockSpec((n_space, 4, LANES), lambda b: (0, 0, 0)),
        ),
        scratch_shapes=[pltpu.VMEM((3 * LANES * 8, LANES), jnp.float32)],
        name="project",
    )(parts, u, h)
    g = lax.all_to_all(blk, SPACE, 0, 0, tiled=True).reshape(n_space * 4, LANES)

    block = rank // 2
    fresh, coherence = pl.pallas_call(
        lambda *refs: update_kernel(nb, rank, *refs),
        grid=(nb, rank // block),
        out_shape=(
            jax.ShapeDtypeStruct(u.shape, jnp.bfloat16),
            jax.ShapeDtypeStruct((nb, 2, rank, rank), jnp.float32),
        ),
        in_specs=[
            smem,
            pl.BlockSpec((n_space * 4, LANES), lambda b, i: (0, 0)),
            pl.BlockSpec((nb, rank), lambda b, i: (0, 0)),
            pl.BlockSpec((1, 2, rows, LANES), lambda b, i: (b, 0, 0, 0)),
            pl.BlockSpec((1, 2, block, rows, LANES), lambda b, i: (b, 0, i, 0, 0)),
        ],
        out_specs=(
            pl.BlockSpec((1, 2, block, rows, LANES), lambda b, i: (b, 0, i, 0, 0)),
            pl.BlockSpec((nb, 2, rank, rank), lambda b, i: (0, 0, 0, 0)),
        ),
        scratch_shapes=[pltpu.VMEM((3 * nb * rank, LANES), jnp.float32)],
        name="update",
    )(block_count, g, eigenvalues, spec, u)
    return unfold(fresh, 3), coherence


def solution(mesh):
    inner = Mesh(mesh.devices.reshape(4, 4, 8, 2), ("ta",) + SPACE)
    return jax.shard_map(
        local,
        mesh=inner,
        in_specs=(P("ta", None, SPACE), P(), P("ta", None), P("ta", None, None, None, SPACE), P()),
        out_specs=(P("ta", None, None, None, SPACE), P("ta", None, None, None)),
        check_vma=False,
    )
```

```python
import math

import jax
import jax.numpy as jnp
import numpy as np
from jax import lax
from jax.experimental import pallas as pl
from jax.experimental.pallas import tpu as pltpu
from jax.sharding import Mesh, PartitionSpec as P

SPACE = ("y", "z", "core")
LANES = 128
BLK = 8
UP = ((2, 0), (2, 1), (1, 2), (1, 3))
DOWN = ((2, 2), (2, 3), (3, 0), (3, 1))
KEEP = ((1, 0), (1, 1), (3, 2), (3, 3))
OWN = ((0, 0), (0, 1), (0, 2), (0, 3))
ORDER = UP + DOWN + KEEP + OWN


def fold(v, axis):
    shape = v.shape
    lead, tiles = shape[:-2], shape[-1] // LANES
    v = v.reshape(*lead, 2, tiles, LANES)
    return jnp.swapaxes(v, axis, axis + 1).reshape(*lead, 2 * tiles, LANES)


def unfold(v, axis):
    lead, rows = v.shape[:-2], v.shape[-2]
    v = v.reshape(*lead, rows // 2, 2, LANES)
    return jnp.swapaxes(v, axis, axis + 1).reshape(*lead, 2, rows // 2 * LANES)


def split3(v):
    hi = v.astype(jnp.bfloat16)
    rest = v - hi.astype(jnp.float32)
    mid = rest.astype(jnp.bfloat16)
    low = (rest - mid.astype(jnp.float32)).astype(jnp.bfloat16)
    return hi, mid, low


def transform_kernel(total, slice_len, rows, bins_ref, place_ref, x_ref, *out_refs):
    n = 2 * len(ORDER)
    place = place_ref[0]
    row = lax.broadcasted_iota(jnp.int32, (n, slice_len), 0)
    t = lax.broadcasted_iota(jnp.int32, (n, slice_len), 1) + place * slice_len
    which = jnp.zeros((n, slice_len), jnp.int32)
    for i, (ahead, b) in enumerate(ORDER):
        which = jnp.where(row // 2 == i, bins_ref[((place + ahead) % 4) * 4 + b], which)
    phase = (which * t + (row % 2) * (total // 4)) % total
    step = 2.0 * math.pi / total
    window = 0.5 - 0.5 * jnp.cos(step * t.astype(jnp.float32))
    table = jnp.cos(step * phase.astype(jnp.float32)) * window * math.sqrt(8.0 / (3.0 * total))
    t_hi = table.astype(jnp.bfloat16)
    t_lo = (table - t_hi.astype(jnp.float32)).astype(jnp.bfloat16)
    left = jnp.concatenate([t_hi, t_lo], axis=0)
    left = jnp.concatenate([left, left], axis=1)
    each = n // len(out_refs)
    for r in range(0, rows, 2):
        x = jnp.concatenate(
            [x_ref[pl.ds(r, slice_len, stride=rows), :], x_ref[pl.ds(r + 1, slice_len, stride=rows), :]],
            axis=1,
        )
        hi = x.astype(jnp.bfloat16)
        lo = (x - hi.astype(jnp.float32)).astype(jnp.bfloat16)
        res = jnp.dot(left, jnp.concatenate([hi, lo], axis=0), preferred_element_type=jnp.float32)
        res = res[:n] + res[n:]
        for i, out_ref in enumerate(out_refs):
            part = res[i * each:(i + 1) * each]
            out_ref[pl.ds(r, each, stride=rows), :] = part[:, :LANES]
            out_ref[pl.ds(r + 1, each, stride=rows), :] = part[:, LANES:]


def gram_kernel(nb, rank, core_ref, u_ref, send_ref, keep_ref, wide_ref, all_ref):
    b = pl.program_id(0)
    rows = u_ref.shape[-2]
    for c in range(2):
        def widen(j, carry, c=c):
            at = pl.multiple_of((c * rank + j) * rows, rows)
            wide_ref[pl.ds(at, rows), :] = u_ref[0, c, j].astype(jnp.float32)
            return carry

        lax.fori_loop(0, rank, widen, 0, unroll=4)
    some = 8
    n = 2 * rank

    def body(i, acc):
        part = [wide_ref[pl.ds(i * some + k, n, stride=rows), :].astype(jnp.bfloat16) for k in range(some)]
        v = jnp.concatenate(part, axis=1)
        return acc + lax.dot_general(v, v, (((1,), (1,)), ((), ())), preferred_element_type=jnp.float32)

    vv = lax.fori_loop(0, rows // some, body, jnp.zeros((n, n), jnp.float32))
    h_re = vv[:rank, :rank] + vv[rank:, rank:]
    h_im = vv[:rank, rank:] - vv[rank:, :rank]
    j = lax.broadcasted_iota(jnp.int32, (rank, rank), 0)
    k = lax.broadcasted_iota(jnp.int32, (rank, rank), 1)
    all_ref[b] = jnp.where(j <= k, h_re, h_im)

    @pl.when(b == nb - 1)
    def _():
        h = jnp.concatenate([all_ref[i] for i in range(nb)], axis=1)
        low, high = h[:rank // 2], h[rank // 2:]
        first = core_ref[0] == 0
        send_ref[...] = jnp.where(first, high, low)
        keep_ref[...] = jnp.where(first, low, high)


def project_kernel(nb, rank, own_ref, a_ref, b_ref, c_ref, d_ref, u_ref, h_ref, s_ref, blk_ref, acc_ref):
    b = pl.program_id(0)
    rows = u_ref.shape[-2]

    @pl.when(b == 0)
    def _():
        acc_ref[...] = jnp.zeros_like(acc_ref)

    low = b < nb // 2
    s = own_ref[0] + jnp.where(low, b_ref[0, 0], a_ref[0, 0]) + jnp.where(low, c_ref[0], d_ref[0])
    s_ref[0] = s
    s_re, s_im = s[0], s[1]

    def eight(v):
        return v.reshape(rows // 8, 8, LANES).sum(axis=0)

    acc_ref[pl.ds((2 * nb * rank + b) * 8, 8), :] = eight(s_re * s_re + s_im * s_im)

    def body(j, carry):
        u_re = u_ref[0, 0, j].astype(jnp.float32)
        u_im = u_ref[0, 1, j].astype(jnp.float32)
        at = (b * 2 * rank + j) * 8
        acc_ref[pl.ds(pl.multiple_of(at, 8), 8), :] = eight(u_re * s_re + u_im * s_im)
        acc_ref[pl.ds(pl.multiple_of(at + rank * 8, 8), 8), :] = eight(u_re * s_im - u_im * s_re)
        return carry

    lax.fori_loop(0, rank, body, 0, unroll=4)

    @pl.when(b == nb - 1)
    def _():
        n = acc_ref.shape[0] // 8
        x = acc_ref[pl.ds(0, n, stride=8), :]
        for k in range(1, 8):
            x = x + acc_ref[pl.ds(k, n, stride=8), :]
        ones = jnp.ones((8, LANES), jnp.bfloat16)
        sums = sum(
            lax.dot_general(ones, v, (((1,), (1,)), ((), ())), preferred_element_type=jnp.float32)
            for v in split3(x)
        )
        blk = jnp.concatenate(
            [sums[0:1, k * LANES:(k + 1) * LANES] for k in range(3)]
            + [h_ref[...], jnp.zeros((1, LANES), jnp.float32)],
            axis=0,
        )
        blk_ref[...] = jnp.broadcast_to(blk[None], blk_ref.shape)


def update_kernel(nb, rank, count_ref, g_ref, pick_ref, eig_ref, s_ref, u_ref, out_ref, coh_ref, coef_ref):
    b, half = pl.program_id(0), pl.program_id(1)
    rows = u_ref.shape[-2]

    @pl.when((b == 0) & (half == 0))
    def _():
        count = jnp.full((1, 1), count_ref[0], jnp.int32).astype(jnp.float32)
        w_old = count / (count + 1.0)
        w_new = 1.0 / (count + 1.0)
        pick = pick_ref[...]
        sums = sum(jnp.dot(pick, v, preferred_element_type=jnp.float32) for v in split3(g_ref[...]))
        g = sums[BLK:]
        g_t = g.T
        j = lax.broadcasted_iota(jnp.int32, (rank, rank), 0)
        k = lax.broadcasted_iota(jnp.int32, (rank, rank), 1)
        eye = j == k

        def col(v):
            return jnp.where(eye, v, 0.0).sum(axis=1, keepdims=True)

        for i in range(nb):
            at = (i % 2) * 2 * rank
            cr = sums[i // 2:i // 2 + 1, at:at + rank]
            ci = sums[i // 2:i // 2 + 1, at + rank:at + 2 * rank]
            power = sums[2:3, i:i + 1]
            a = w_old * eig_ref[i:i + 1, :]
            cr_c, ci_c, a_c = col(cr), col(ci), col(a)
            p = g[:, i * rank:(i + 1) * rank]
            p_t = g_t[i * rank:(i + 1) * rank, :]
            h_re = jnp.where(j <= k, p, p_t)
            h_im = jnp.where(j > k, p, jnp.where(eye, 0.0, -p_t))
            both = w_new * (a_c + a + w_new * power)
            gram_re = a_c * a * h_re + (cr_c * cr + ci_c * ci) * both
            gram_im = a_c * a * h_im + (ci_c * cr - cr_c * ci) * both
            diag = jnp.where(eye, gram_re, 0.0)
            inv_c = 1.0 / jnp.sqrt(diag.sum(axis=1, keepdims=True) + 1e-06)
            inv_r = 1.0 / jnp.sqrt(diag.sum(axis=0, keepdims=True) + 1e-06)
            coh_ref[i, 0] = gram_re * inv_c * inv_r
            coh_ref[i, 1] = gram_im * inv_c * inv_r
            for m, v in enumerate((a_c * inv_c, w_new * cr_c * inv_c, w_new * ci_c * inv_c)):
                coef_ref[pl.ds((m * nb + i) * rank, rank), :] = jnp.broadcast_to(v, (rank, LANES))

    s_re, s_im = s_ref[0, 0], s_ref[0, 1]
    block = u_ref.shape[2]

    def body(j, carry):
        at = b * rank + half * block + j

        def coef(m):
            one = coef_ref[pl.ds(m * nb * rank + at, 1), :]
            return jnp.broadcast_to(one, (rows, LANES))

        alpha, beta, gamma = coef(0), coef(1), coef(2)
        u_re = u_ref[0, 0, j].astype(jnp.float32)
        u_im = u_ref[0, 1, j].astype(jnp.float32)
        out_ref[0, 0, j] = (alpha * u_re + (beta * s_re + gamma * s_im)).astype(out_ref.dtype)
        out_ref[0, 1, j] = (alpha * u_im + (beta * s_im - gamma * s_re)).astype(out_ref.dtype)
        return carry

    lax.fori_loop(0, block, body, 0, unroll=4)


def pick_table(rank):
    m = np.zeros((BLK + rank, 64 * BLK), np.float32)
    for s in range(64):
        y, core = s // 16, s % 2
        for k in range(3):
            m[k, s * BLK + k] = 1.0
        for i in range(4):
            m[BLK + core * 16 + (y & 1) * 8 + (y >> 1) * 4 + i, s * BLK + 3 + i] = 1.0
    return jnp.asarray(m, jnp.bfloat16)


def trade(v, axis, mask):
    n = lax.axis_size(axis)
    return lax.ppermute(v, axis, [(i, i ^ mask) for i in range(n)])


SMEM = pl.BlockSpec(memory_space=pltpu.SMEM)
VMEM = pl.BlockSpec(memory_space=pltpu.VMEM)


def call_transform(bins, place, x, total, slice_len, rows):
    n = 2 * len(ORDER)
    return pl.pallas_call(
        lambda *refs: transform_kernel(total, slice_len, rows, *refs),
        out_shape=[jax.ShapeDtypeStruct((n // 4 * rows, LANES), jnp.float32)] * 4,
        in_specs=[SMEM, SMEM, VMEM],
        out_specs=[VMEM] * 4,
        name="transform",
    )(bins, place, x)


def call_gram(core, u):
    nb, _, rank, rows, _ = u.shape
    return pl.pallas_call(
        lambda *refs: gram_kernel(nb, rank, *refs),
        grid=(nb,),
        out_shape=[jax.ShapeDtypeStruct((rank // 2, nb * rank), jnp.float32)] * 2,
        in_specs=[SMEM, pl.BlockSpec((1, 2, rank, rows, LANES), lambda b: (b, 0, 0, 0, 0))],
        out_specs=[pl.BlockSpec((rank // 2, nb * rank), lambda b: (0, 0))] * 2,
        scratch_shapes=[
            pltpu.VMEM((2 * rank * rows, LANES), jnp.float32),
            pltpu.VMEM((nb, rank, rank), jnp.float32),
        ],
        cost_estimate=pl.CostEstimate(flops=2 * nb * (2 * rank) ** 2 * rows * LANES * 8, bytes_accessed=u.size * 4, transcendentals=0),
        name="gram",
    )(core, u)


def call_project(own, a, b_, c, d, u, h, n_space):
    nb, _, rank, rows, _ = u.shape
    half = nb // 2
    return pl.pallas_call(
        lambda *refs: project_kernel(nb, rank, *refs),
        grid=(nb,),
        out_shape=(
            jax.ShapeDtypeStruct((nb, 2, rows, LANES), jnp.float32),
            jax.ShapeDtypeStruct((n_space, BLK, LANES), jnp.float32),
        ),
        in_specs=[
            pl.BlockSpec((1, 2, rows, LANES), lambda b: (b, 0, 0, 0)),
            pl.BlockSpec((1, 1, 2, rows, LANES), lambda b: (1, jnp.maximum(b - half, 0), 0, 0, 0)),
            pl.BlockSpec((1, 1, 2, rows, LANES), lambda b: (1, jnp.minimum(b, half - 1), 0, 0, 0)),
            pl.BlockSpec((1, 2, rows, LANES), lambda b: (jnp.minimum(b, half - 1), 0, 0, 0)),
            pl.BlockSpec((1, 2, rows, LANES), lambda b: (jnp.maximum(b - half, 0), 0, 0, 0)),
            pl.BlockSpec((1, 2, rank, rows, LANES), lambda b: (b, 0, 0, 0, 0)),
            pl.BlockSpec((4, LANES), lambda b: (0, 0)),
        ],
        out_specs=(
            pl.BlockSpec((1, 2, rows, LANES), lambda b: (b, 0, 0, 0)),
            pl.BlockSpec((n_space, BLK, LANES), lambda b: (0, 0, 0)),
        ),
        scratch_shapes=[pltpu.VMEM((3 * LANES * 8, LANES), jnp.float32)],
        cost_estimate=pl.CostEstimate(flops=16 * u.size, bytes_accessed=u.size * 2, transcendentals=0),
        name="project",
    )(own, a, b_, c, d, u, h)


def call_update(block_count, g, eigenvalues, spec, u):
    nb, _, rank, rows, _ = u.shape
    block = rank // 2
    n = g.shape[0]
    return pl.pallas_call(
        lambda *refs: update_kernel(nb, rank, *refs),
        grid=(nb, rank // block),
        out_shape=(
            jax.ShapeDtypeStruct(u.shape, jnp.bfloat16),
            jax.ShapeDtypeStruct((nb, 2, rank, rank), jnp.float32),
        ),
        in_specs=[
            SMEM,
            pl.BlockSpec((n, LANES), lambda b, i: (0, 0)),
            pl.BlockSpec((BLK + rank, n), lambda b, i: (0, 0)),
            pl.BlockSpec((nb, rank), lambda b, i: (0, 0)),
            pl.BlockSpec((1, 2, rows, LANES), lambda b, i: (b, 0, 0, 0)),
            pl.BlockSpec((1, 2, block, rows, LANES), lambda b, i: (b, 0, i, 0, 0)),
        ],
        out_specs=(
            pl.BlockSpec((1, 2, block, rows, LANES), lambda b, i: (b, 0, i, 0, 0)),
            pl.BlockSpec((nb, 2, rank, rank), lambda b, i: (0, 0, 0, 0)),
        ),
        scratch_shapes=[pltpu.VMEM((3 * nb * rank, LANES), jnp.float32)],
        name="update",
    )(block_count, g, pick_table(rank), eigenvalues, spec, u)


def local(snapshots, bins, eigenvalues, old_basis, block_count):
    slice_len, _, points = snapshots.shape
    groups = lax.axis_size("ta")
    total = slice_len * groups
    rows = 2 * points // LANES
    nb, _, rank = old_basis.shape[:3]
    n_space = lax.axis_size(SPACE)
    place = lax.axis_index("ta").astype(jnp.int32).reshape(1)
    core = lax.axis_index("core").astype(jnp.int32).reshape(1)
    y = lax.axis_index("y")

    x = fold(snapshots, 1).reshape(slice_len * rows, LANES)
    up, down, keep, own = call_transform(bins, place, x, total, slice_len, rows)
    ring_up = [(i, (i + 1) % groups) for i in range(groups)]
    ring_down = [(i, (i - 1) % groups) for i in range(groups)]
    a = lax.ppermute(up, "ta", ring_up)
    b = lax.ppermute(down, "ta", ring_down)

    u = fold(old_basis, 3)
    send, kept = call_gram(core, u)
    h = kept + trade(send, "core", 1)

    half = up.shape[0] // 2
    c = lax.ppermute(keep[:half] + a[:half], "ta", ring_up)
    d = lax.ppermute(keep[half:] + b[:half], "ta", ring_down)

    for bit in (0, 1):
        n = h.shape[0] // 2
        first = (y >> bit) & 1 == 0
        h = jnp.where(first, h[:n], h[n:]) + trade(jnp.where(first, h[n:], h[:n]), "y", 1 << bit)

    spec, blk = call_project(
        own.reshape(nb, 2, rows, LANES),
        a.reshape(2, nb // 2, 2, rows, LANES),
        b.reshape(2, nb // 2, 2, rows, LANES),
        c.reshape(nb // 2, 2, rows, LANES),
        d.reshape(nb // 2, 2, rows, LANES),
        u, h, n_space,
    )
    g = lax.all_to_all(blk, SPACE, 0, 0, tiled=True).reshape(n_space * BLK, LANES)
    fresh, coherence = call_update(block_count, g, eigenvalues, spec, u)
    return unfold(fresh, 3), coherence


def solution(mesh):
    inner = Mesh(mesh.devices.reshape(4, 4, 8, 2), ("ta",) + SPACE)
    return jax.shard_map(
        local,
        mesh=inner,
        in_specs=(P("ta", None, SPACE), P(), P("ta", None), P("ta", None, None, None, SPACE), P()),
        out_specs=(P("ta", None, None, None, SPACE), P("ta", None, None, None)),
        check_vma=False,
    )
```

```python
import math

import jax
import jax.numpy as jnp
import numpy as np
from jax import lax
from jax.experimental import pallas as pl
from jax.experimental.pallas import tpu as pltpu
from jax.sharding import Mesh, PartitionSpec as P

SPACE = ("y", "z", "core")
LANES = 128
BLK = 8
UP = ((2, 0), (2, 1), (1, 2), (1, 3))
DOWN = ((2, 2), (2, 3), (3, 0), (3, 1))
KEEP = ((1, 0), (1, 1), (3, 2), (3, 3))
OWN = ((0, 0), (0, 1), (0, 2), (0, 3))
ORDER = UP + DOWN + KEEP + OWN


def fold(v, axis):
    shape = v.shape
    lead, tiles = shape[:-2], shape[-1] // LANES
    v = v.reshape(*lead, 2, tiles, LANES)
    return jnp.swapaxes(v, axis, axis + 1).reshape(*lead, 2 * tiles, LANES)


def unfold(v, axis):
    lead, rows = v.shape[:-2], v.shape[-2]
    v = v.reshape(*lead, rows // 2, 2, LANES)
    return jnp.swapaxes(v, axis, axis + 1).reshape(*lead, 2, rows // 2 * LANES)


def split3(v):
    hi = v.astype(jnp.bfloat16)
    rest = v - hi.astype(jnp.float32)
    mid = rest.astype(jnp.bfloat16)
    low = (rest - mid.astype(jnp.float32)).astype(jnp.bfloat16)
    return hi, mid, low


def transform_kernel(total, chunks, bins_ref, place_ref, x_hbm, *refs):
    *out_refs, x_ref, sems = refs
    slice_len, rows, _ = x_ref.shape
    piece = rows // chunks
    copies = [
        pltpu.make_async_copy(x_hbm.at[:, pl.ds(c * piece, piece)], x_ref.at[:, pl.ds(c * piece, piece)], sems.at[c])
        for c in range(chunks)
    ]
    for copy in copies:
        copy.start()
    n = 2 * len(ORDER)
    place = place_ref[0]
    row = lax.broadcasted_iota(jnp.int32, (n, slice_len), 0)
    t = lax.broadcasted_iota(jnp.int32, (n, slice_len), 1) + place * slice_len
    which = jnp.zeros((n, slice_len), jnp.int32)
    for i, (ahead, b) in enumerate(ORDER):
        which = jnp.where(row // 2 == i, bins_ref[((place + ahead) % 4) * 4 + b], which)
    phase = (which * t + (row % 2) * (total // 4)) % total
    step = 2.0 * math.pi / total
    window = 0.5 - 0.5 * jnp.cos(step * t.astype(jnp.float32))
    table = jnp.cos(step * phase.astype(jnp.float32)) * window * math.sqrt(8.0 / (3.0 * total))
    t_hi = table.astype(jnp.bfloat16)
    t_lo = (table - t_hi.astype(jnp.float32)).astype(jnp.bfloat16)
    left = jnp.concatenate([t_hi, t_lo], axis=0)
    left = jnp.concatenate([left, left], axis=1)
    each = n // len(out_refs)
    for at in range(0, rows, 8):
        if at % piece == 0:
            copies[at // piece].wait()
        x8 = jnp.swapaxes(x_ref[:, at:at + 8, :], 0, 1)
        got = []
        for r in range(0, 8, 2):
            x = jnp.concatenate([x8[r], x8[r + 1]], axis=1)
            hi = x.astype(jnp.bfloat16)
            lo = (x - hi.astype(jnp.float32)).astype(jnp.bfloat16)
            res = jnp.dot(left, jnp.concatenate([hi, lo], axis=0), preferred_element_type=jnp.float32)
            res = res[:n] + res[n:]
            got += [res[:, :LANES], res[:, LANES:]]
        got = jnp.swapaxes(jnp.stack(got, axis=0), 0, 1)
        for i, out_ref in enumerate(out_refs):
            out_ref[:, at:at + 8, :] = got[i * each:(i + 1) * each]


def gram_kernel(core_ref, u_hbm, send_ref, keep_ref, all_ref, u_ref, sems):
    nb, _, rank, rows, _ = u_ref.shape
    n = 2 * rank

    def load(b):
        return pltpu.make_async_copy(u_hbm.at[b], u_ref.at[b], sems.at[b])

    for b in range(nb):
        load(b).start()

    def one(b, carry):
        load(b).wait()
        vv = jnp.zeros((n, n), jnp.float32)
        for at in range(0, rows, 16):
            u = u_ref[b, :, :, at:at + 16, :].reshape(n, 16, LANES)
            u = jnp.swapaxes(u, 0, 1)
            for r in range(0, 16, 4):
                v = jnp.concatenate([u[r + k] for k in range(4)], axis=1)
                vv = vv + lax.dot_general(v, v, (((1,), (1,)), ((), ())), preferred_element_type=jnp.float32)
        h_re = vv[:rank, :rank] + vv[rank:, rank:]
        h_im = vv[:rank, rank:] - vv[rank:, :rank]
        j = lax.broadcasted_iota(jnp.int32, (rank, rank), 0)
        k = lax.broadcasted_iota(jnp.int32, (rank, rank), 1)
        all_ref[b] = jnp.where(j <= k, h_re, h_im)
        return carry

    lax.fori_loop(0, nb, one, 0)
    h = jnp.concatenate([all_ref[i] for i in range(nb)], axis=1)
    low, high = h[:rank // 2], h[rank // 2:]
    first = core_ref[0] == 0
    send_ref[...] = jnp.where(first, high, low)
    keep_ref[...] = jnp.where(first, low, high)


def project_kernel(own_ref, a_ref, b_ref, c_ref, d_ref, u_hbm, h_ref, s_ref, blk_ref, acc_ref, u_ref, sems):
    nb, _, rank, rows, _ = u_ref.shape
    loads = [pltpu.make_async_copy(u_hbm.at[b], u_ref.at[b], sems.at[b]) for b in range(nb)]
    for load in loads:
        load.start()
    half = nb // 2
    used = nb * (2 * rank + 1) * 8
    acc_ref[pl.ds(used, acc_ref.shape[0] - used), :] = jnp.zeros((acc_ref.shape[0] - used, LANES), jnp.float32)

    def eight(v):
        return v.reshape(rows // 8, 8, LANES).sum(axis=0)

    for b in range(nb):
        at = 2 * b
        s = []
        for k in (at, at + 1):
            if b < half:
                s.append(own_ref[k] + b_ref[k + nb] + c_ref[k])
            else:
                s.append(own_ref[k] + a_ref[k] + d_ref[k - nb])
        s_re, s_im = s
        s_ref[b, 0] = s_re
        s_ref[b, 1] = s_im
        acc_ref[pl.ds((2 * nb * rank + b) * 8, 8), :] = eight(s_re * s_re + s_im * s_im)
        loads[b].wait()

        def body(j, carry, b=b, s_re=s_re, s_im=s_im):
            u_re = u_ref[b, 0, j].astype(jnp.float32)
            u_im = u_ref[b, 1, j].astype(jnp.float32)
            at = (b * 2 * rank + j) * 8
            acc_ref[pl.ds(pl.multiple_of(at, 8), 8), :] = eight(u_re * s_re + u_im * s_im)
            acc_ref[pl.ds(pl.multiple_of(at + rank * 8, 8), 8), :] = eight(u_re * s_im - u_im * s_re)
            return carry

        lax.fori_loop(0, rank, body, 0, unroll=4)

    n = acc_ref.shape[0] // 8
    x = acc_ref[pl.ds(0, n, stride=8), :]
    for k in range(1, 8):
        x = x + acc_ref[pl.ds(k, n, stride=8), :]
    ones = jnp.ones((8, LANES), jnp.bfloat16)
    sums = sum(
        lax.dot_general(ones, v, (((1,), (1,)), ((), ())), preferred_element_type=jnp.float32)
        for v in split3(x)
    )
    blk = jnp.concatenate(
        [sums[0:1, k * LANES:(k + 1) * LANES] for k in range(3)]
        + [h_ref[...], jnp.zeros((1, LANES), jnp.float32)],
        axis=0,
    )
    blk_ref[...] = jnp.broadcast_to(blk[None], blk_ref.shape)


def update_kernel(parts, count_ref, g_ref, pick_ref, eig_ref, s_ref, u_hbm, out_hbm, coh_ref, coef_ref, u_ref, out_ref, in_sems, sems):
    nb, _, rank, rows, _ = u_ref.shape
    loads = [pltpu.make_async_copy(u_hbm.at[b], u_ref.at[b], in_sems.at[b]) for b in range(nb)]
    for load in loads:
        load.start()

    def coefficients():
        count = jnp.full((1, 1), count_ref[0], jnp.int32).astype(jnp.float32)
        w_old = count / (count + 1.0)
        w_new = 1.0 / (count + 1.0)
        pick = pick_ref[...]
        sums = sum(jnp.dot(pick, v, preferred_element_type=jnp.float32) for v in split3(g_ref[...]))
        g = sums[BLK:]
        g_t = g.T
        j = lax.broadcasted_iota(jnp.int32, (rank, rank), 0)
        k = lax.broadcasted_iota(jnp.int32, (rank, rank), 1)
        eye = j == k

        def col(v):
            return jnp.where(eye, v, 0.0).sum(axis=1, keepdims=True)

        for i in range(nb):
            at = (i % 2) * 2 * rank
            cr = sums[i // 2:i // 2 + 1, at:at + rank]
            ci = sums[i // 2:i // 2 + 1, at + rank:at + 2 * rank]
            power = sums[2:3, i:i + 1]
            a = w_old * eig_ref[i:i + 1, :]
            cr_c, ci_c, a_c = col(cr), col(ci), col(a)
            p = g[:, i * rank:(i + 1) * rank]
            p_t = g_t[i * rank:(i + 1) * rank, :]
            h_re = jnp.where(j <= k, p, p_t)
            h_im = jnp.where(j > k, p, jnp.where(eye, 0.0, -p_t))
            both = w_new * (a_c + a + w_new * power)
            gram_re = a_c * a * h_re + (cr_c * cr + ci_c * ci) * both
            gram_im = a_c * a * h_im + (ci_c * cr - cr_c * ci) * both
            diag = jnp.where(eye, gram_re, 0.0)
            inv_c = 1.0 / jnp.sqrt(diag.sum(axis=1, keepdims=True) + 1e-06)
            inv_r = 1.0 / jnp.sqrt(diag.sum(axis=0, keepdims=True) + 1e-06)
            coh_ref[i, 0] = gram_re * inv_c * inv_r
            coh_ref[i, 1] = gram_im * inv_c * inv_r
            for m, v in enumerate((a_c * inv_c, w_new * cr_c * inv_c, w_new * ci_c * inv_c)):
                coef_ref[pl.ds((m * nb + i) * rank, rank), :] = jnp.broadcast_to(v, (rank, LANES))

    coefficients()
    block = rank // parts
    copies = []
    for b in range(nb):
        loads[b].wait()
        s_re, s_im = s_ref[b, 0], s_ref[b, 1]

        def body(j, carry, b=b, s_re=s_re, s_im=s_im):
            def coef(m):
                one = coef_ref[pl.ds((m * nb + b) * rank + j, 1), :]
                return jnp.broadcast_to(one, (rows, LANES))

            alpha, beta, gamma = coef(0), coef(1), coef(2)
            u_re = u_ref[b, 0, j].astype(jnp.float32)
            u_im = u_ref[b, 1, j].astype(jnp.float32)
            out_ref[b, 0, j] = (alpha * u_re + (beta * s_re + gamma * s_im)).astype(out_ref.dtype)
            out_ref[b, 1, j] = (alpha * u_im + (beta * s_im - gamma * s_re)).astype(out_ref.dtype)
            return carry

        for part in range(parts):
            lax.fori_loop(part * block, (part + 1) * block, body, 0, unroll=4)
            at = pl.ds(part * block, block)
            copy = pltpu.make_async_copy(out_ref.at[b, :, at], out_hbm.at[b, :, at], sems.at[b * parts + part])
            copy.start()
            copies.append(copy)
    for copy in copies:
        copy.wait()


def pick_table(rank):
    m = np.zeros((BLK + rank, 64 * BLK), np.float32)
    for s in range(64):
        y, core = s // 16, s % 2
        for k in range(3):
            m[k, s * BLK + k] = 1.0
        for i in range(4):
            m[BLK + core * 16 + y * 4 + i, s * BLK + 3 + i] = 1.0
    return jnp.asarray(m, jnp.bfloat16)


def trade(v, axis, mask):
    n = lax.axis_size(axis)
    return lax.ppermute(v, axis, [(i, i ^ mask) for i in range(n)])


SMEM = pl.BlockSpec(memory_space=pltpu.SMEM)
VMEM = pl.BlockSpec(memory_space=pltpu.VMEM)
HBM = pl.BlockSpec(memory_space=pltpu.HBM)


def room(kib):
    return pltpu.CompilerParams(vmem_limit_bytes=kib * 1024)


def call_transform(bins, place, x, total, chunks=4):
    slice_len, rows, _ = x.shape
    n = 2 * len(ORDER)
    return pl.pallas_call(
        lambda *refs: transform_kernel(total, chunks, *refs),
        out_shape=[jax.ShapeDtypeStruct((n // 4, rows, LANES), jnp.float32)] * 4,
        in_specs=[SMEM, SMEM, HBM],
        out_specs=[VMEM] * 4,
        scratch_shapes=[pltpu.VMEM(x.shape, jnp.float32), pltpu.SemaphoreType.DMA((chunks,))],
        compiler_params=room(53500),
        name="transform",
    )(bins, place, x)


def call_gram(core, u):
    nb, _, rank, rows, _ = u.shape
    return pl.pallas_call(
        gram_kernel,
        out_shape=[jax.ShapeDtypeStruct((rank // 2, nb * rank), jnp.float32)] * 2,
        in_specs=[SMEM, HBM],
        out_specs=[VMEM] * 2,
        scratch_shapes=[
            pltpu.VMEM((nb, rank, rank), jnp.float32),
            pltpu.VMEM(u.shape, u.dtype),
            pltpu.SemaphoreType.DMA((nb,)),
        ],
        compiler_params=room(52000),
        cost_estimate=pl.CostEstimate(flops=4 * 10**9, bytes_accessed=u.size * 2, transcendentals=0),
        name="gram",
    )(core, u)


def call_project(own, a, b, c, d, u, h, n_space):
    nb, _, rank, rows, _ = u.shape
    return pl.pallas_call(
        project_kernel,
        out_shape=(
            jax.ShapeDtypeStruct((nb, 2, rows, LANES), jnp.float32),
            jax.ShapeDtypeStruct((n_space, BLK, LANES), jnp.float32),
        ),
        in_specs=[VMEM] * 5 + [HBM, VMEM],
        out_specs=(VMEM, VMEM),
        scratch_shapes=[
            pltpu.VMEM((3 * LANES * 8, LANES), jnp.float32),
            pltpu.VMEM(u.shape, u.dtype),
            pltpu.SemaphoreType.DMA((nb,)),
        ],
        compiler_params=room(52000),
        cost_estimate=pl.CostEstimate(flops=16 * u.size, bytes_accessed=u.size * 2, transcendentals=0),
        name="project",
    )(own, a, b, c, d, u, h)


def call_update(block_count, g, eigenvalues, spec, u, parts=2):
    nb, _, rank, rows, _ = u.shape
    return pl.pallas_call(
        lambda *refs: update_kernel(parts, *refs),
        out_shape=(
            jax.ShapeDtypeStruct(u.shape, jnp.bfloat16),
            jax.ShapeDtypeStruct((nb, 2, rank, rank), jnp.float32),
        ),
        in_specs=[SMEM] + [VMEM] * 4 + [HBM],
        out_specs=(HBM, VMEM),
        scratch_shapes=[
            pltpu.VMEM((3 * nb * rank, LANES), jnp.float32),
            pltpu.VMEM(u.shape, u.dtype),
            pltpu.VMEM(u.shape, u.dtype),
            pltpu.SemaphoreType.DMA((nb,)),
            pltpu.SemaphoreType.DMA((nb * parts,)),
        ],
        compiler_params=room(52000),
        name="update",
    )(block_count, g, pick_table(rank), eigenvalues, spec, u)


def local(snapshots, bins, eigenvalues, old_basis, block_count):
    slice_len = snapshots.shape[0]
    groups = lax.axis_size("ta")
    total = slice_len * groups
    nb = old_basis.shape[0]
    n_space = lax.axis_size(SPACE)
    place = lax.axis_index("ta").astype(jnp.int32).reshape(1)
    core = lax.axis_index("core").astype(jnp.int32).reshape(1)
    y = lax.axis_index("y")

    up, down, keep, own = call_transform(bins, place, fold(snapshots, 1), total)
    ring_up = [(i, (i + 1) % groups) for i in range(groups)]
    ring_down = [(i, (i - 1) % groups) for i in range(groups)]
    a = lax.ppermute(up, "ta", ring_up)
    b = lax.ppermute(down, "ta", ring_down)

    u = fold(old_basis, 3)
    u, _ = lax.optimization_barrier((u, up))
    send, kept = call_gram(core, u)

    h = kept + trade(send, "core", 1)

    c, d = keep[:nb] + a[:nb], keep[nb:] + b[:nb]
    c, d, h = lax.optimization_barrier((c, d, h))
    c = lax.ppermute(c, "ta", ring_up)
    d = lax.ppermute(d, "ta", ring_down)

    n = h.shape[0] // 4
    h = h.reshape(4, n, h.shape[1])
    quarter = [lax.dynamic_index_in_dim(h, y ^ k, 0, keepdims=False) for k in range(4)]
    h = quarter[0] + trade(quarter[1], "y", 1) + trade(quarter[2], "y", 2) + trade(quarter[3], "y", 3)

    spec, blk = call_project(own, a, b, c, d, u, h, n_space)
    g = lax.all_to_all(blk, SPACE, 0, 0, tiled=True).reshape(n_space * BLK, LANES)
    fresh, coherence = call_update(block_count, g, eigenvalues, spec, u)
    return unfold(fresh, 3), coherence


def solution(mesh):
    inner = Mesh(mesh.devices.reshape(4, 4, 8, 2), ("ta",) + SPACE)
    return jax.shard_map(
        local,
        mesh=inner,
        in_specs=(P("ta", None, SPACE), P(), P("ta", None), P("ta", None, None, None, SPACE), P()),
        out_specs=(P("ta", None, None, None, SPACE), P("ta", None, None, None)),
        check_vma=False,
    )
```

```python
import math

import jax
import jax.numpy as jnp
import numpy as np
from jax import lax
from jax.experimental import pallas as pl
from jax.experimental.pallas import tpu as pltpu
from jax.sharding import Mesh, PartitionSpec as P

SPACE = ("y", "z", "core")
LANES = 128
BLK = 4
UP = ((2, 0), (2, 1), (1, 2), (1, 3))
DOWN = ((2, 2), (2, 3), (3, 0), (3, 1))
KEEP = ((1, 0), (1, 1), (3, 2), (3, 3))
OWN = ((0, 0), (0, 1), (0, 2), (0, 3))
ORDER = UP + DOWN + KEEP + OWN


def fold(v, axis):
    shape = v.shape
    lead, tiles = shape[:-2], shape[-1] // LANES
    v = v.reshape(*lead, 2, tiles, LANES)
    return jnp.swapaxes(v, axis, axis + 1).reshape(*lead, 2 * tiles, LANES)


def unfold(v, axis):
    lead, rows = v.shape[:-2], v.shape[-2]
    v = v.reshape(*lead, rows // 2, 2, LANES)
    return jnp.swapaxes(v, axis, axis + 1).reshape(*lead, 2, rows // 2 * LANES)


def split3(v):
    hi = v.astype(jnp.bfloat16)
    rest = v - hi.astype(jnp.float32)
    mid = rest.astype(jnp.bfloat16)
    low = (rest - mid.astype(jnp.float32)).astype(jnp.bfloat16)
    return hi, mid, low


def transform_kernel(total, chunks, bins_ref, place_ref, x_hbm, *refs):
    *out_refs, x_ref, sems = refs
    slice_len, rows, _ = x_ref.shape
    piece = rows // chunks
    copies = [
        pltpu.make_async_copy(x_hbm.at[:, pl.ds(c * piece, piece)], x_ref.at[:, pl.ds(c * piece, piece)], sems.at[c])
        for c in range(chunks)
    ]
    for copy in copies:
        copy.start()
    n = 2 * len(ORDER)
    place = place_ref[0]
    row = lax.broadcasted_iota(jnp.int32, (n, slice_len), 0)
    t = lax.broadcasted_iota(jnp.int32, (n, slice_len), 1) + place * slice_len
    which = jnp.zeros((n, slice_len), jnp.int32)
    for i, (ahead, b) in enumerate(ORDER):
        which = jnp.where(row // 2 == i, bins_ref[((place + ahead) % 4) * 4 + b], which)
    phase = (which * t + (row % 2) * (total // 4)) % total
    step = 2.0 * math.pi / total
    window = 0.5 - 0.5 * jnp.cos(step * t.astype(jnp.float32))
    table = jnp.cos(step * phase.astype(jnp.float32)) * window * math.sqrt(8.0 / (3.0 * total))
    t_hi = table.astype(jnp.bfloat16)
    t_lo = (table - t_hi.astype(jnp.float32)).astype(jnp.bfloat16)
    left = jnp.concatenate([t_hi, t_lo], axis=0)
    left = jnp.concatenate([left, left], axis=1)
    each = n // len(out_refs)
    for at in range(0, rows, 8):
        if at % piece == 0:
            copies[at // piece].wait()
        x8 = jnp.swapaxes(x_ref[:, at:at + 8, :], 0, 1)
        got = []
        for r in range(0, 8, 2):
            x = jnp.concatenate([x8[r], x8[r + 1]], axis=1)
            hi = x.astype(jnp.bfloat16)
            lo = (x - hi.astype(jnp.float32)).astype(jnp.bfloat16)
            res = jnp.dot(left, jnp.concatenate([hi, lo], axis=0), preferred_element_type=jnp.float32)
            res = res[:n] + res[n:]
            got += [res[:, :LANES], res[:, LANES:]]
        got = jnp.swapaxes(jnp.stack(got, axis=0), 0, 1)
        for i, out_ref in enumerate(out_refs):
            out_ref[:, at:at + 8, :] = got[i * each:(i + 1) * each]


def gram_kernel(u_hbm, h_ref, all_ref, u_ref, sems):
    nb, _, rank, rows, _ = u_ref.shape
    n = 2 * rank

    def load(b):
        return pltpu.make_async_copy(u_hbm.at[b], u_ref.at[b], sems.at[b])

    for b in range(nb):
        load(b).start()

    def one(b, carry):
        load(b).wait()
        vv = jnp.zeros((n, n), jnp.float32)
        for at in range(0, rows, 16):
            u = u_ref[b, :, :, at:at + 16, :].reshape(n, 16, LANES)
            u = jnp.swapaxes(u, 0, 1)
            for r in range(0, 16, 4):
                v = jnp.concatenate([u[r + k] for k in range(4)], axis=1)
                vv = vv + lax.dot_general(v, v, (((1,), (1,)), ((), ())), preferred_element_type=jnp.float32)
        h_re = vv[:rank, :rank] + vv[rank:, rank:]
        h_im = vv[:rank, rank:] - vv[rank:, :rank]
        j = lax.broadcasted_iota(jnp.int32, (rank, rank), 0)
        k = lax.broadcasted_iota(jnp.int32, (rank, rank), 1)
        all_ref[b] = jnp.where(j <= k, h_re, h_im)
        return carry

    lax.fori_loop(0, nb, one, 0)
    h_ref[...] = jnp.concatenate([all_ref[i] for i in range(nb)], axis=1)


def project_kernel(own_ref, a_ref, b_ref, c_ref, d_ref, u_hbm, h_ref, s_ref, blk_ref, acc_ref, u_ref, sems):
    nb, _, rank, rows, _ = u_ref.shape
    loads = [pltpu.make_async_copy(u_hbm.at[b], u_ref.at[b], sems.at[b]) for b in range(nb)]
    for load in loads:
        load.start()
    half = nb // 2
    used = nb * (2 * rank + 1) * 8
    acc_ref[pl.ds(used, acc_ref.shape[0] - used), :] = jnp.zeros((acc_ref.shape[0] - used, LANES), jnp.float32)

    def eight(v):
        return v.reshape(rows // 8, 8, LANES).sum(axis=0)

    for b in range(nb):
        at = 2 * b
        s = []
        for k in (at, at + 1):
            if b < half:
                s.append(own_ref[k] + b_ref[k + nb] + c_ref[k])
            else:
                s.append(own_ref[k] + a_ref[k] + d_ref[k - nb])
        s_re, s_im = s
        s_ref[b, 0] = s_re
        s_ref[b, 1] = s_im
        acc_ref[pl.ds((2 * nb * rank + b) * 8, 8), :] = eight(s_re * s_re + s_im * s_im)
        loads[b].wait()

        def body(j, carry, b=b, s_re=s_re, s_im=s_im):
            u_re = u_ref[b, 0, j].astype(jnp.float32)
            u_im = u_ref[b, 1, j].astype(jnp.float32)
            at = (b * 2 * rank + j) * 8
            acc_ref[pl.ds(pl.multiple_of(at, 8), 8), :] = eight(u_re * s_re + u_im * s_im)
            acc_ref[pl.ds(pl.multiple_of(at + rank * 8, 8), 8), :] = eight(u_re * s_im - u_im * s_re)
            return carry

        lax.fori_loop(0, rank, body, 0, unroll=4)

    n = acc_ref.shape[0] // 8
    x = acc_ref[pl.ds(0, n, stride=8), :]
    for k in range(1, 8):
        x = x + acc_ref[pl.ds(k, n, stride=8), :]
    ones = jnp.ones((8, LANES), jnp.bfloat16)
    sums = sum(
        lax.dot_general(ones, v, (((1,), (1,)), ((), ())), preferred_element_type=jnp.float32)
        for v in split3(x)
    )
    blk = jnp.concatenate(
        [sums[0:1, k * LANES:(k + 1) * LANES] for k in range(3)]
        + [h_ref[...].sum(axis=0, keepdims=True)],
        axis=0,
    )
    blk_ref[...] = jnp.broadcast_to(blk[None], blk_ref.shape)


def update_kernel(parts, count_ref, g_ref, pick_ref, eig_ref, s_ref, u_hbm, out_hbm, coh_ref, coef_ref, u_ref, out_ref, in_sems, sems):
    nb, _, rank, rows, _ = u_ref.shape
    loads = [pltpu.make_async_copy(u_hbm.at[b], u_ref.at[b], in_sems.at[b]) for b in range(nb)]
    for load in loads:
        load.start()

    def coefficients():
        count = jnp.full((1, 1), count_ref[0], jnp.int32).astype(jnp.float32)
        w_old = count / (count + 1.0)
        w_new = 1.0 / (count + 1.0)
        pick = pick_ref[...]
        sums = sum(jnp.dot(pick, v, preferred_element_type=jnp.float32) for v in split3(g_ref[...]))
        g = sums[8:]
        g_t = g.T
        j = lax.broadcasted_iota(jnp.int32, (rank, rank), 0)
        k = lax.broadcasted_iota(jnp.int32, (rank, rank), 1)
        eye = j == k

        def col(v):
            return jnp.where(eye, v, 0.0).sum(axis=1, keepdims=True)

        for i in range(nb):
            at = (i % 2) * 2 * rank
            cr = sums[i // 2:i // 2 + 1, at:at + rank]
            ci = sums[i // 2:i // 2 + 1, at + rank:at + 2 * rank]
            power = sums[2:3, i:i + 1]
            a = w_old * eig_ref[i:i + 1, :]
            cr_c, ci_c, a_c = col(cr), col(ci), col(a)
            p = g[:, i * rank:(i + 1) * rank]
            p_t = g_t[i * rank:(i + 1) * rank, :]
            h_re = jnp.where(j <= k, p, p_t)
            h_im = jnp.where(j > k, p, jnp.where(eye, 0.0, -p_t))
            both = w_new * (a_c + a + w_new * power)
            gram_re = a_c * a * h_re + (cr_c * cr + ci_c * ci) * both
            gram_im = a_c * a * h_im + (ci_c * cr - cr_c * ci) * both
            diag = jnp.where(eye, gram_re, 0.0)
            inv_c = 1.0 / jnp.sqrt(diag.sum(axis=1, keepdims=True) + 1e-06)
            inv_r = 1.0 / jnp.sqrt(diag.sum(axis=0, keepdims=True) + 1e-06)
            coh_ref[i, 0] = gram_re * inv_c * inv_r
            coh_ref[i, 1] = gram_im * inv_c * inv_r
            for m, v in enumerate((a_c * inv_c, w_new * cr_c * inv_c, w_new * ci_c * inv_c)):
                coef_ref[pl.ds((m * nb + i) * rank, rank), :] = jnp.broadcast_to(v, (rank, LANES))

    coefficients()
    block = rank // parts
    copies = []
    for b in range(nb):
        loads[b].wait()
        s_re, s_im = s_ref[b, 0], s_ref[b, 1]

        def body(j, carry, b=b, s_re=s_re, s_im=s_im):
            def coef(m):
                one = coef_ref[pl.ds((m * nb + b) * rank + j, 1), :]
                return jnp.broadcast_to(one, (rows, LANES))

            alpha, beta, gamma = coef(0), coef(1), coef(2)
            u_re = u_ref[b, 0, j].astype(jnp.float32)
            u_im = u_ref[b, 1, j].astype(jnp.float32)
            out_ref[b, 0, j] = (alpha * u_re + (beta * s_re + gamma * s_im)).astype(out_ref.dtype)
            out_ref[b, 1, j] = (alpha * u_im + (beta * s_im - gamma * s_re)).astype(out_ref.dtype)
            return carry

        for part in range(parts):
            lax.fori_loop(part * block, (part + 1) * block, body, 0, unroll=4)
            at = pl.ds(part * block, block)
            copy = pltpu.make_async_copy(out_ref.at[b, :, at], out_hbm.at[b, :, at], sems.at[b * parts + part])
            copy.start()
            copies.append(copy)
    for copy in copies:
        copy.wait()


def pick_table(rank, n_space):
    m = np.zeros((8 + rank, n_space * BLK), np.float32)
    for s in range(n_space):
        for k in range(3):
            m[k, s * BLK + k] = 1.0
        m[8 + s * rank // n_space, s * BLK + 3] = 1.0
    return jnp.asarray(m, jnp.bfloat16)


SMEM = pl.BlockSpec(memory_space=pltpu.SMEM)
VMEM = pl.BlockSpec(memory_space=pltpu.VMEM)
HBM = pl.BlockSpec(memory_space=pltpu.HBM)


def room(kib):
    return pltpu.CompilerParams(vmem_limit_bytes=kib * 1024)


def call_transform(bins, place, x, total, chunks=4):
    slice_len, rows, _ = x.shape
    n = 2 * len(ORDER)
    return pl.pallas_call(
        lambda *refs: transform_kernel(total, chunks, *refs),
        out_shape=[jax.ShapeDtypeStruct((n // 4, rows, LANES), jnp.float32)] * 4,
        in_specs=[SMEM, SMEM, HBM],
        out_specs=[VMEM] * 4,
        scratch_shapes=[pltpu.VMEM(x.shape, jnp.float32), pltpu.SemaphoreType.DMA((chunks,))],
        compiler_params=room(53500),
        name="transform",
    )(bins, place, x)


def call_gram(u):
    nb, _, rank, rows, _ = u.shape
    return pl.pallas_call(
        gram_kernel,
        out_shape=jax.ShapeDtypeStruct((rank, nb * rank), jnp.float32),
        in_specs=[HBM],
        out_specs=VMEM,
        scratch_shapes=[
            pltpu.VMEM((nb, rank, rank), jnp.float32),
            pltpu.VMEM(u.shape, u.dtype),
            pltpu.SemaphoreType.DMA((nb,)),
        ],
        compiler_params=room(52000),
        cost_estimate=pl.CostEstimate(flops=4 * 10**9, bytes_accessed=u.size * 2, transcendentals=0),
        name="gram",
    )(u)


def call_project(own, a, b, c, d, u, h, n_space):
    nb, _, rank, rows, _ = u.shape
    return pl.pallas_call(
        project_kernel,
        out_shape=(
            jax.ShapeDtypeStruct((nb, 2, rows, LANES), jnp.float32),
            jax.ShapeDtypeStruct((n_space, BLK, LANES), jnp.float32),
        ),
        in_specs=[VMEM] * 5 + [HBM, VMEM],
        out_specs=(VMEM, VMEM),
        scratch_shapes=[
            pltpu.VMEM((3 * LANES * 8, LANES), jnp.float32),
            pltpu.VMEM(u.shape, u.dtype),
            pltpu.SemaphoreType.DMA((nb,)),
        ],
        compiler_params=room(52000),
        cost_estimate=pl.CostEstimate(flops=16 * u.size, bytes_accessed=u.size * 2, transcendentals=0),
        name="project",
    )(own, a, b, c, d, u, h)


def call_update(block_count, g, eigenvalues, spec, u, parts=2):
    nb, _, rank, rows, _ = u.shape
    return pl.pallas_call(
        lambda *refs: update_kernel(parts, *refs),
        out_shape=(
            jax.ShapeDtypeStruct(u.shape, jnp.bfloat16),
            jax.ShapeDtypeStruct((nb, 2, rank, rank), jnp.float32),
        ),
        in_specs=[SMEM] + [VMEM] * 4 + [HBM],
        out_specs=(HBM, VMEM),
        scratch_shapes=[
            pltpu.VMEM((3 * nb * rank, LANES), jnp.float32),
            pltpu.VMEM(u.shape, u.dtype),
            pltpu.VMEM(u.shape, u.dtype),
            pltpu.SemaphoreType.DMA((nb,)),
            pltpu.SemaphoreType.DMA((nb * parts,)),
        ],
        compiler_params=room(52000),
        name="update",
    )(block_count, g, pick_table(rank, g.shape[0] // BLK), eigenvalues, spec, u)


def local(snapshots, bins, eigenvalues, old_basis, block_count):
    slice_len = snapshots.shape[0]
    groups = lax.axis_size("ta")
    total = slice_len * groups
    nb = old_basis.shape[0]
    n_space = lax.axis_size(SPACE)
    place = lax.axis_index("ta").astype(jnp.int32).reshape(1)

    up, down, keep, own = call_transform(bins, place, fold(snapshots, 1), total)
    ring_up = [(i, (i + 1) % groups) for i in range(groups)]
    ring_down = [(i, (i - 1) % groups) for i in range(groups)]
    a = lax.ppermute(up, "ta", ring_up)
    b = lax.ppermute(down, "ta", ring_down)

    u = fold(old_basis, 3)
    u, _ = lax.optimization_barrier((u, up))
    h = call_gram(u)
    c, d = keep[:nb] + a[:nb], keep[nb:] + b[:nb]
    c, d, h = lax.optimization_barrier((c, d, h))
    c = lax.ppermute(c, "ta", ring_up)
    d = lax.ppermute(d, "ta", ring_down)
    h = lax.all_to_all(h[:, None], ("y", "z"), 0, 0, tiled=True)[:, 0]

    spec, blk = call_project(own, a, b, c, d, u, h, n_space)
    g = lax.all_to_all(blk, SPACE, 0, 0, tiled=True).reshape(n_space * BLK, LANES)
    fresh, coherence = call_update(block_count, g, eigenvalues, spec, u)
    return unfold(fresh, 3), coherence


def solution(mesh):
    inner = Mesh(mesh.devices.reshape(4, 4, 8, 2), ("ta",) + SPACE)
    return jax.shard_map(
        local,
        mesh=inner,
        in_specs=(P("ta", None, SPACE), P(), P("ta", None), P("ta", None, None, None, SPACE), P()),
        out_specs=(P("ta", None, None, None, SPACE), P("ta", None, None, None)),
        check_vma=False,
    )
```

```python
import math

import jax
import jax.numpy as jnp
import numpy as np
from jax import lax
from jax.experimental import pallas as pl
from jax.experimental.pallas import tpu as pltpu
from jax.sharding import Mesh, PartitionSpec as P

SPACE = ("y", "z", "core")
LANES = 128
BLK = 8
UP = ((2, 0), (2, 1), (1, 2), (1, 3))
DOWN = ((2, 2), (2, 3), (3, 0), (3, 1))
KEEP = ((1, 0), (1, 1), (3, 2), (3, 3))
OWN = ((0, 0), (0, 1), (0, 2), (0, 3))
ORDER = UP + DOWN + KEEP + OWN


def fold(v, axis):
    shape = v.shape
    lead, tiles = shape[:-2], shape[-1] // LANES
    v = v.reshape(*lead, 2, tiles, LANES)
    return jnp.swapaxes(v, axis, axis + 1).reshape(*lead, 2 * tiles, LANES)


def unfold(v, axis):
    lead, rows = v.shape[:-2], v.shape[-2]
    v = v.reshape(*lead, rows // 2, 2, LANES)
    return jnp.swapaxes(v, axis, axis + 1).reshape(*lead, 2, rows // 2 * LANES)


def split3(v):
    hi = v.astype(jnp.bfloat16)
    rest = v - hi.astype(jnp.float32)
    mid = rest.astype(jnp.bfloat16)
    low = (rest - mid.astype(jnp.float32)).astype(jnp.bfloat16)
    return hi, mid, low


def transform_kernel(total, chunks, bins_ref, place_ref, x_hbm, *refs):
    *out_refs, x_ref, sems = refs
    slice_len, rows, _ = x_ref.shape
    piece = rows // chunks
    copies = [
        pltpu.make_async_copy(x_hbm.at[:, pl.ds(c * piece, piece)], x_ref.at[:, pl.ds(c * piece, piece)], sems.at[c])
        for c in range(chunks)
    ]
    for copy in copies:
        copy.start()
    n = 2 * len(ORDER)
    place = place_ref[0]
    row = lax.broadcasted_iota(jnp.int32, (n, slice_len), 0)
    t = lax.broadcasted_iota(jnp.int32, (n, slice_len), 1) + place * slice_len
    which = jnp.zeros((n, slice_len), jnp.int32)
    for i, (ahead, b) in enumerate(ORDER):
        which = jnp.where(row // 2 == i, bins_ref[((place + ahead) % 4) * 4 + b], which)
    phase = (which * t + (row % 2) * (total // 4)) % total
    step = 2.0 * math.pi / total
    window = 0.5 - 0.5 * jnp.cos(step * t.astype(jnp.float32))
    table = jnp.cos(step * phase.astype(jnp.float32)) * window * math.sqrt(8.0 / (3.0 * total))
    t_hi = table.astype(jnp.bfloat16)
    t_lo = (table - t_hi.astype(jnp.float32)).astype(jnp.bfloat16)
    left = jnp.concatenate([t_hi, t_lo], axis=0)
    left = jnp.concatenate([left, left], axis=1)
    each = n // len(out_refs)
    for at in range(0, rows, 8):
        if at % piece == 0:
            copies[at // piece].wait()
        x8 = jnp.swapaxes(x_ref[:, at:at + 8, :], 0, 1)
        got = []
        for r in range(0, 8, 2):
            x = jnp.concatenate([x8[r], x8[r + 1]], axis=1)
            hi = x.astype(jnp.bfloat16)
            lo = (x - hi.astype(jnp.float32)).astype(jnp.bfloat16)
            res = jnp.dot(left, jnp.concatenate([hi, lo], axis=0), preferred_element_type=jnp.float32)
            res = res[:n] + res[n:]
            got += [res[:, :LANES], res[:, LANES:]]
        got = jnp.swapaxes(jnp.stack(got, axis=0), 0, 1)
        for i, out_ref in enumerate(out_refs):
            out_ref[:, at:at + 8, :] = got[i * each:(i + 1) * each]


def gram_kernel(core_ref, u_hbm, send_ref, keep_ref, all_ref, u_ref, sems):
    nb, _, rank, rows, _ = u_ref.shape
    n = 2 * rank

    def load(b):
        return pltpu.make_async_copy(u_hbm.at[b], u_ref.at[b], sems.at[b])

    for b in range(nb):
        load(b).start()

    def one(b, carry):
        load(b).wait()
        vv = jnp.zeros((n, n), jnp.float32)
        for at in range(0, rows, 16):
            u = u_ref[b, :, :, at:at + 16, :].reshape(n, 16, LANES)
            u = jnp.swapaxes(u, 0, 1)
            for r in range(0, 16, 4):
                v = jnp.concatenate([u[r + k] for k in range(4)], axis=1)
                vv = vv + lax.dot_general(v, v, (((1,), (1,)), ((), ())), preferred_element_type=jnp.float32)
        h_re = vv[:rank, :rank] + vv[rank:, rank:]
        h_im = vv[:rank, rank:] - vv[rank:, :rank]
        j = lax.broadcasted_iota(jnp.int32, (rank, rank), 0)
        k = lax.broadcasted_iota(jnp.int32, (rank, rank), 1)
        all_ref[b] = jnp.where(j <= k, h_re, h_im)
        return carry

    lax.fori_loop(0, nb, one, 0)
    h = jnp.concatenate([all_ref[i] for i in range(nb)], axis=1)
    low, high = h[:rank // 2], h[rank // 2:]
    first = core_ref[0] == 0
    send_ref[...] = jnp.where(first, high, low)
    keep_ref[...] = jnp.where(first, low, high)


def project_kernel(own_ref, a_ref, b_ref, c_ref, d_ref, u_hbm, h0_ref, h1_ref, h2_ref, h3_ref, s_ref, blk_ref, acc_ref, u_ref, sems):
    nb, _, rank, rows, _ = u_ref.shape
    loads = [pltpu.make_async_copy(u_hbm.at[b], u_ref.at[b], sems.at[b]) for b in range(nb)]
    for load in loads:
        load.start()
    half = nb // 2
    used = nb * (2 * rank + 1) * 8
    acc_ref[pl.ds(used, acc_ref.shape[0] - used), :] = jnp.zeros((acc_ref.shape[0] - used, LANES), jnp.float32)

    def eight(v):
        return v.reshape(rows // 8, 8, LANES).sum(axis=0)

    for b in range(nb):
        at = 2 * b
        s = []
        for k in (at, at + 1):
            if b < half:
                s.append(own_ref[k] + b_ref[k + nb] + c_ref[k])
            else:
                s.append(own_ref[k] + a_ref[k] + d_ref[k - nb])
        s_re, s_im = s
        s_ref[b, 0] = s_re
        s_ref[b, 1] = s_im
        acc_ref[pl.ds((2 * nb * rank + b) * 8, 8), :] = eight(s_re * s_re + s_im * s_im)
        loads[b].wait()

        def body(j, carry, b=b, s_re=s_re, s_im=s_im):
            u_re = u_ref[b, 0, j].astype(jnp.float32)
            u_im = u_ref[b, 1, j].astype(jnp.float32)
            at = (b * 2 * rank + j) * 8
            acc_ref[pl.ds(pl.multiple_of(at, 8), 8), :] = eight(u_re * s_re + u_im * s_im)
            acc_ref[pl.ds(pl.multiple_of(at + rank * 8, 8), 8), :] = eight(u_re * s_im - u_im * s_re)
            return carry

        lax.fori_loop(0, rank, body, 0, unroll=4)

    n = acc_ref.shape[0] // 8
    x = acc_ref[pl.ds(0, n, stride=8), :]
    for k in range(1, 8):
        x = x + acc_ref[pl.ds(k, n, stride=8), :]
    ones = jnp.ones((8, LANES), jnp.bfloat16)
    sums = sum(
        lax.dot_general(ones, v, (((1,), (1,)), ((), ())), preferred_element_type=jnp.float32)
        for v in split3(x)
    )
    blk = jnp.concatenate(
        [sums[0:1, k * LANES:(k + 1) * LANES] for k in range(3)]
        + [h0_ref[...] + h1_ref[...] + h2_ref[...] + h3_ref[...], jnp.zeros((1, LANES), jnp.float32)],
        axis=0,
    )
    blk_ref[...] = jnp.broadcast_to(blk[None], blk_ref.shape)


def update_kernel(parts, count_ref, g_ref, pick_ref, eig_ref, s_ref, u_hbm, out_hbm, coh_ref, coef_ref, u_ref, out_ref, in_sems, sems):
    nb, _, rank, rows, _ = u_ref.shape
    loads = [pltpu.make_async_copy(u_hbm.at[b], u_ref.at[b], in_sems.at[b]) for b in range(nb)]
    for load in loads:
        load.start()

    def coefficients():
        count = jnp.full((1, 1), count_ref[0], jnp.int32).astype(jnp.float32)
        w_old = count / (count + 1.0)
        w_new = 1.0 / (count + 1.0)
        pick = pick_ref[...]
        sums = sum(jnp.dot(pick, v, preferred_element_type=jnp.float32) for v in split3(g_ref[...]))
        g = sums[BLK:]
        g_t = g.T
        j = lax.broadcasted_iota(jnp.int32, (rank, rank), 0)
        k = lax.broadcasted_iota(jnp.int32, (rank, rank), 1)
        eye = j == k

        def col(v):
            return jnp.where(eye, v, 0.0).sum(axis=1, keepdims=True)

        for i in range(nb):
            at = (i % 2) * 2 * rank
            cr = sums[i // 2:i // 2 + 1, at:at + rank]
            ci = sums[i // 2:i // 2 + 1, at + rank:at + 2 * rank]
            power = sums[2:3, i:i + 1]
            a = w_old * eig_ref[i:i + 1, :]
            cr_c, ci_c, a_c = col(cr), col(ci), col(a)
            p = g[:, i * rank:(i + 1) * rank]
            p_t = g_t[i * rank:(i + 1) * rank, :]
            h_re = jnp.where(j <= k, p, p_t)
            h_im = jnp.where(j > k, p, jnp.where(eye, 0.0, -p_t))
            both = w_new * (a_c + a + w_new * power)
            gram_re = a_c * a * h_re + (cr_c * cr + ci_c * ci) * both
            gram_im = a_c * a * h_im + (ci_c * cr - cr_c * ci) * both
            diag = jnp.where(eye, gram_re, 0.0)
            inv_c = 1.0 / jnp.sqrt(diag.sum(axis=1, keepdims=True) + 1e-06)
            inv_r = 1.0 / jnp.sqrt(diag.sum(axis=0, keepdims=True) + 1e-06)
            coh_ref[i, 0] = gram_re * inv_c * inv_r
            coh_ref[i, 1] = gram_im * inv_c * inv_r
            for m, v in enumerate((a_c * inv_c, w_new * cr_c * inv_c, w_new * ci_c * inv_c)):
                coef_ref[pl.ds((m * nb + i) * rank, rank), :] = jnp.broadcast_to(v, (rank, LANES))

    coefficients()
    block = rank // parts
    copies = []
    for b in range(nb):
        loads[b].wait()
        s_re, s_im = s_ref[b, 0], s_ref[b, 1]

        def body(j, carry, b=b, s_re=s_re, s_im=s_im):
            def coef(m):
                one = coef_ref[pl.ds((m * nb + b) * rank + j, 1), :]
                return jnp.broadcast_to(one, (rows, LANES))

            alpha, beta, gamma = coef(0), coef(1), coef(2)
            u_re = u_ref[b, 0, j].astype(jnp.float32)
            u_im = u_ref[b, 1, j].astype(jnp.float32)
            out_ref[b, 0, j] = (alpha * u_re + (beta * s_re + gamma * s_im)).astype(out_ref.dtype)
            out_ref[b, 1, j] = (alpha * u_im + (beta * s_im - gamma * s_re)).astype(out_ref.dtype)
            return carry

        for part in range(parts):
            lax.fori_loop(part * block, (part + 1) * block, body, 0, unroll=4)
            at = pl.ds(part * block, block)
            copy = pltpu.make_async_copy(out_ref.at[b, :, at], out_hbm.at[b, :, at], sems.at[b * parts + part])
            copy.start()
            copies.append(copy)
    for copy in copies:
        copy.wait()


def pick_table(rank):
    m = np.zeros((BLK + rank, 64 * BLK), np.float32)
    for s in range(64):
        y, core = s // 16, s % 2
        for k in range(3):
            m[k, s * BLK + k] = 1.0
        for i in range(4):
            m[BLK + core * 16 + y * 4 + i, s * BLK + 3 + i] = 1.0
    return jnp.asarray(m, jnp.bfloat16)


def trade(v, axis, mask):
    n = lax.axis_size(axis)
    return lax.ppermute(v, axis, [(i, i ^ mask) for i in range(n)])


SMEM = pl.BlockSpec(memory_space=pltpu.SMEM)
VMEM = pl.BlockSpec(memory_space=pltpu.VMEM)
HBM = pl.BlockSpec(memory_space=pltpu.HBM)


def room(kib):
    return pltpu.CompilerParams(vmem_limit_bytes=kib * 1024)


def call_transform(bins, place, x, total, chunks=4):
    slice_len, rows, _ = x.shape
    n = 2 * len(ORDER)
    return pl.pallas_call(
        lambda *refs: transform_kernel(total, chunks, *refs),
        out_shape=[jax.ShapeDtypeStruct((n // 4, rows, LANES), jnp.float32)] * 4,
        in_specs=[SMEM, SMEM, HBM],
        out_specs=[VMEM] * 4,
        scratch_shapes=[pltpu.VMEM(x.shape, jnp.float32), pltpu.SemaphoreType.DMA((chunks,))],
        compiler_params=room(53500),
        name="transform",
    )(bins, place, x)


def call_gram(core, u):
    nb, _, rank, rows, _ = u.shape
    return pl.pallas_call(
        gram_kernel,
        out_shape=[jax.ShapeDtypeStruct((rank // 2, nb * rank), jnp.float32)] * 2,
        in_specs=[SMEM, HBM],
        out_specs=[VMEM] * 2,
        scratch_shapes=[
            pltpu.VMEM((nb, rank, rank), jnp.float32),
            pltpu.VMEM(u.shape, u.dtype),
            pltpu.SemaphoreType.DMA((nb,)),
        ],
        compiler_params=room(52000),
        cost_estimate=pl.CostEstimate(flops=4 * 10**9, bytes_accessed=u.size * 2, transcendentals=0),
        name="gram",
    )(core, u)


def call_project(own, a, b, c, d, u, h, n_space):
    nb, _, rank, rows, _ = u.shape
    return pl.pallas_call(
        project_kernel,
        out_shape=(
            jax.ShapeDtypeStruct((nb, 2, rows, LANES), jnp.float32),
            jax.ShapeDtypeStruct((n_space, BLK, LANES), jnp.float32),
        ),
        in_specs=[VMEM] * 5 + [HBM] + [VMEM] * 4,
        out_specs=(VMEM, VMEM),
        scratch_shapes=[
            pltpu.VMEM((3 * LANES * 8, LANES), jnp.float32),
            pltpu.VMEM(u.shape, u.dtype),
            pltpu.SemaphoreType.DMA((nb,)),
        ],
        compiler_params=room(52000),
        cost_estimate=pl.CostEstimate(flops=16 * u.size, bytes_accessed=u.size * 2, transcendentals=0),
        name="project",
    )(own, a, b, c, d, u, *h)


def call_update(block_count, g, eigenvalues, spec, u, parts=2):
    nb, _, rank, rows, _ = u.shape
    return pl.pallas_call(
        lambda *refs: update_kernel(parts, *refs),
        out_shape=(
            jax.ShapeDtypeStruct(u.shape, jnp.bfloat16),
            jax.ShapeDtypeStruct((nb, 2, rank, rank), jnp.float32),
        ),
        in_specs=[SMEM] + [VMEM] * 4 + [HBM],
        out_specs=(HBM, VMEM),
        scratch_shapes=[
            pltpu.VMEM((3 * nb * rank, LANES), jnp.float32),
            pltpu.VMEM(u.shape, u.dtype),
            pltpu.VMEM(u.shape, u.dtype),
            pltpu.SemaphoreType.DMA((nb,)),
            pltpu.SemaphoreType.DMA((nb * parts,)),
        ],
        compiler_params=room(52000),
        name="update",
    )(block_count, g, pick_table(rank), eigenvalues, spec, u)


def local(snapshots, bins, eigenvalues, old_basis, block_count):
    slice_len = snapshots.shape[0]
    groups = lax.axis_size("ta")
    total = slice_len * groups
    nb = old_basis.shape[0]
    n_space = lax.axis_size(SPACE)
    place = lax.axis_index("ta").astype(jnp.int32).reshape(1)
    core = lax.axis_index("core").astype(jnp.int32).reshape(1)
    y = lax.axis_index("y")

    up, down, keep, own = call_transform(bins, place, fold(snapshots, 1), total)
    ring_up = [(i, (i + 1) % groups) for i in range(groups)]
    ring_down = [(i, (i - 1) % groups) for i in range(groups)]
    a = lax.ppermute(up, "ta", ring_up)
    b = lax.ppermute(down, "ta", ring_down)

    u = fold(old_basis, 3)
    u, _ = lax.optimization_barrier((u, up))
    send, kept = call_gram(core, u)

    h = kept + trade(send, "core", 1)

    c, d = keep[:nb] + a[:nb], keep[nb:] + b[:nb]
    c, d, h = lax.optimization_barrier((c, d, h))
    c = lax.ppermute(c, "ta", ring_up)
    d = lax.ppermute(d, "ta", ring_down)

    n = h.shape[0] // 4
    h = h.reshape(4, n, h.shape[1])
    h = [lax.dynamic_index_in_dim(h, y ^ k, 0, keepdims=False) for k in range(4)]
    h = [h[0]] + [trade(h[k], "y", k) for k in (1, 2, 3)]
    spec, blk = call_project(own, a, b, c, d, u, h, n_space)
    g = lax.all_to_all(blk, SPACE, 0, 0, tiled=True).reshape(n_space * BLK, LANES)
    fresh, coherence = call_update(block_count, g, eigenvalues, spec, u)
    return unfold(fresh, 3), coherence


def solution(mesh):
    inner = Mesh(mesh.devices.reshape(4, 4, 8, 2), ("ta",) + SPACE)
    return jax.shard_map(
        local,
        mesh=inner,
        in_specs=(P("ta", None, SPACE), P(), P("ta", None), P("ta", None, None, None, SPACE), P()),
        out_specs=(P("ta", None, None, None, SPACE), P("ta", None, None, None)),
        check_vma=False,
    )
```

```python
import math

import jax
import jax.numpy as jnp
import numpy as np
from jax import lax
from jax.experimental import pallas as pl
from jax.experimental.pallas import tpu as pltpu
from jax.sharding import Mesh, PartitionSpec as P

SPACE = ("y", "z", "core")
LANES = 128
BLK = 8

def fold(v, axis):
    shape = v.shape
    lead, tiles = shape[:-2], shape[-1] // LANES
    v = v.reshape(*lead, 2, tiles, LANES)
    return jnp.swapaxes(v, axis, axis + 1).reshape(*lead, 2 * tiles, LANES)


def unfold(v, axis):
    lead, rows = v.shape[:-2], v.shape[-2]
    v = v.reshape(*lead, rows // 2, 2, LANES)
    return jnp.swapaxes(v, axis, axis + 1).reshape(*lead, 2, rows // 2 * LANES)


def split3(v):
    hi = v.astype(jnp.bfloat16)
    rest = v - hi.astype(jnp.float32)
    mid = rest.astype(jnp.bfloat16)
    low = (rest - mid.astype(jnp.float32)).astype(jnp.bfloat16)
    return hi, mid, low


def transform_kernel(total, chunks, bins_ref, place_ref, x_hbm, out_ref, x_ref, sems):
    slice_len, rows, _ = x_ref.shape
    piece = rows // chunks
    copies = [
        pltpu.make_async_copy(x_hbm.at[:, pl.ds(c * piece, piece)], x_ref.at[:, pl.ds(c * piece, piece)], sems.at[c])
        for c in range(chunks)
    ]
    for copy in copies:
        copy.start()
    n = 2 * bins_ref.shape[0]
    place = place_ref[0]
    row = lax.broadcasted_iota(jnp.int32, (n, slice_len), 0)
    t = lax.broadcasted_iota(jnp.int32, (n, slice_len), 1) + place * slice_len
    which = jnp.zeros((n, slice_len), jnp.int32)
    for i in range(n // 2):
        which = jnp.where(row // 2 == i, bins_ref[i], which)
    phase = (which * t + (row % 2) * (total // 4)) % total
    step = 2.0 * math.pi / total
    window = 0.5 - 0.5 * jnp.cos(step * t.astype(jnp.float32))
    table = jnp.cos(step * phase.astype(jnp.float32)) * window * math.sqrt(8.0 / (3.0 * total))
    t_hi = table.astype(jnp.bfloat16)
    t_lo = (table - t_hi.astype(jnp.float32)).astype(jnp.bfloat16)
    left = jnp.concatenate([t_hi, t_lo], axis=0)
    left = jnp.concatenate([left, left], axis=1)
    for at in range(0, rows, 8):
        if at % piece == 0:
            copies[at // piece].wait()
        x8 = jnp.swapaxes(x_ref[:, at:at + 8, :], 0, 1)
        got = []
        for r in range(0, 8, 2):
            x = jnp.concatenate([x8[r], x8[r + 1]], axis=1)
            hi = x.astype(jnp.bfloat16)
            lo = (x - hi.astype(jnp.float32)).astype(jnp.bfloat16)
            res = jnp.dot(left, jnp.concatenate([hi, lo], axis=0), preferred_element_type=jnp.float32)
            res = res[:n] + res[n:]
            got += [res[:, :LANES], res[:, LANES:]]
        got = jnp.swapaxes(jnp.stack(got, axis=0), 0, 1)
        out_ref[:, at:at + 8, :] = got


def gram_kernel(core_ref, u_hbm, send_ref, keep_ref, all_ref, u_ref, sems):
    nb, _, rank, rows, _ = u_ref.shape
    n = 2 * rank

    def load(b):
        return pltpu.make_async_copy(u_hbm.at[b], u_ref.at[b], sems.at[b])

    for b in range(nb):
        load(b).start()

    def one(b, carry):
        load(b).wait()
        vv = jnp.zeros((n, n), jnp.float32)
        for at in range(0, rows, 16):
            u = u_ref[b, :, :, at:at + 16, :].reshape(n, 16, LANES)
            u = jnp.swapaxes(u, 0, 1)
            for r in range(0, 16, 4):
                v = jnp.concatenate([u[r + k] for k in range(4)], axis=1)
                vv = vv + lax.dot_general(v, v, (((1,), (1,)), ((), ())), preferred_element_type=jnp.float32)
        h_re = vv[:rank, :rank] + vv[rank:, rank:]
        h_im = vv[:rank, rank:] - vv[rank:, :rank]
        j = lax.broadcasted_iota(jnp.int32, (rank, rank), 0)
        k = lax.broadcasted_iota(jnp.int32, (rank, rank), 1)
        all_ref[b] = jnp.where(j <= k, h_re, h_im)
        return carry

    lax.fori_loop(0, nb, one, 0)
    h = jnp.concatenate([all_ref[i] for i in range(nb)], axis=1)
    low, high = h[:rank // 2], h[rank // 2:]
    first = core_ref[0] == 0
    send_ref[...] = jnp.where(first, high, low)
    keep_ref[...] = jnp.where(first, low, high)


def project_kernel(parts_ref, u_hbm, h0_ref, h1_ref, h2_ref, h3_ref, s_ref, blk_ref, acc_ref, u_ref, sems):
    nb, _, rank, rows, _ = u_ref.shape
    loads = [pltpu.make_async_copy(u_hbm.at[b], u_ref.at[b], sems.at[b]) for b in range(nb)]
    for load in loads:
        load.start()
    used = nb * (2 * rank + 1) * 8
    acc_ref[pl.ds(used, acc_ref.shape[0] - used), :] = jnp.zeros((acc_ref.shape[0] - used, LANES), jnp.float32)

    def eight(v):
        return v.reshape(rows // 8, 8, LANES).sum(axis=0)

    for b in range(nb):
        at = 2 * b
        s = []
        for k in (at, at + 1):
            s.append((parts_ref[0, k] + parts_ref[1, k]) + (parts_ref[2, k] + parts_ref[3, k]))
        s_re, s_im = s
        s_ref[b, 0] = s_re
        s_ref[b, 1] = s_im
        acc_ref[pl.ds((2 * nb * rank + b) * 8, 8), :] = eight(s_re * s_re + s_im * s_im)
        loads[b].wait()

        def body(j, carry, b=b, s_re=s_re, s_im=s_im):
            u_re = u_ref[b, 0, j].astype(jnp.float32)
            u_im = u_ref[b, 1, j].astype(jnp.float32)
            at = (b * 2 * rank + j) * 8
            acc_ref[pl.ds(pl.multiple_of(at, 8), 8), :] = eight(u_re * s_re + u_im * s_im)
            acc_ref[pl.ds(pl.multiple_of(at + rank * 8, 8), 8), :] = eight(u_re * s_im - u_im * s_re)
            return carry

        lax.fori_loop(0, rank, body, 0, unroll=4)

    n = acc_ref.shape[0] // 8
    x = acc_ref[pl.ds(0, n, stride=8), :]
    for k in range(1, 8):
        x = x + acc_ref[pl.ds(k, n, stride=8), :]
    ones = jnp.ones((8, LANES), jnp.bfloat16)
    sums = sum(
        lax.dot_general(ones, v, (((1,), (1,)), ((), ())), preferred_element_type=jnp.float32)
        for v in split3(x)
    )
    blk = jnp.concatenate(
        [sums[0:1, k * LANES:(k + 1) * LANES] for k in range(3)]
        + [h0_ref[...] + h1_ref[...] + h2_ref[...] + h3_ref[...], jnp.zeros((1, LANES), jnp.float32)],
        axis=0,
    )
    blk_ref[...] = jnp.broadcast_to(blk[None], blk_ref.shape)


def update_kernel(parts, count_ref, g_ref, pick_ref, eig_ref, s_ref, u_hbm, out_hbm, coh_ref, coef_ref, u_ref, out_ref, in_sems, sems):
    nb, _, rank, rows, _ = u_ref.shape
    loads = [pltpu.make_async_copy(u_hbm.at[b], u_ref.at[b], in_sems.at[b]) for b in range(nb)]
    for load in loads:
        load.start()

    def coefficients():
        count = jnp.full((1, 1), count_ref[0], jnp.int32).astype(jnp.float32)
        w_old = count / (count + 1.0)
        w_new = 1.0 / (count + 1.0)
        pick = pick_ref[...]
        sums = sum(jnp.dot(pick, v, preferred_element_type=jnp.float32) for v in split3(g_ref[...]))
        g = sums[BLK:]
        g_t = g.T
        j = lax.broadcasted_iota(jnp.int32, (rank, rank), 0)
        k = lax.broadcasted_iota(jnp.int32, (rank, rank), 1)
        eye = j == k

        def col(v):
            return jnp.where(eye, v, 0.0).sum(axis=1, keepdims=True)

        for i in range(nb):
            at = (i % 2) * 2 * rank
            cr = sums[i // 2:i // 2 + 1, at:at + rank]
            ci = sums[i // 2:i // 2 + 1, at + rank:at + 2 * rank]
            power = sums[2:3, i:i + 1]
            a = w_old * eig_ref[i:i + 1, :]
            cr_c, ci_c, a_c = col(cr), col(ci), col(a)
            p = g[:, i * rank:(i + 1) * rank]
            p_t = g_t[i * rank:(i + 1) * rank, :]
            h_re = jnp.where(j <= k, p, p_t)
            h_im = jnp.where(j > k, p, jnp.where(eye, 0.0, -p_t))
            both = w_new * (a_c + a + w_new * power)
            gram_re = a_c * a * h_re + (cr_c * cr + ci_c * ci) * both
            gram_im = a_c * a * h_im + (ci_c * cr - cr_c * ci) * both
            diag = jnp.where(eye, gram_re, 0.0)
            inv_c = 1.0 / jnp.sqrt(diag.sum(axis=1, keepdims=True) + 1e-06)
            inv_r = 1.0 / jnp.sqrt(diag.sum(axis=0, keepdims=True) + 1e-06)
            coh_ref[i, 0] = gram_re * inv_c * inv_r
            coh_ref[i, 1] = gram_im * inv_c * inv_r
            for m, v in enumerate((a_c * inv_c, w_new * cr_c * inv_c, w_new * ci_c * inv_c)):
                coef_ref[pl.ds((m * nb + i) * rank, rank), :] = jnp.broadcast_to(v, (rank, LANES))

    coefficients()
    block = rank // parts
    copies = []
    for b in range(nb):
        loads[b].wait()
        s_re, s_im = s_ref[b, 0], s_ref[b, 1]

        def body(j, carry, b=b, s_re=s_re, s_im=s_im):
            def coef(m):
                one = coef_ref[pl.ds((m * nb + b) * rank + j, 1), :]
                return jnp.broadcast_to(one, (rows, LANES))

            alpha, beta, gamma = coef(0), coef(1), coef(2)
            u_re = u_ref[b, 0, j].astype(jnp.float32)
            u_im = u_ref[b, 1, j].astype(jnp.float32)
            out_ref[b, 0, j] = (alpha * u_re + (beta * s_re + gamma * s_im)).astype(out_ref.dtype)
            out_ref[b, 1, j] = (alpha * u_im + (beta * s_im - gamma * s_re)).astype(out_ref.dtype)
            return carry

        for part in range(parts):
            lax.fori_loop(part * block, (part + 1) * block, body, 0, unroll=4)
            at = pl.ds(part * block, block)
            copy = pltpu.make_async_copy(out_ref.at[b, :, at], out_hbm.at[b, :, at], sems.at[b * parts + part])
            copy.start()
            copies.append(copy)
    for copy in copies:
        copy.wait()


def pick_table(rank):
    m = np.zeros((BLK + rank, 64 * BLK), np.float32)
    for s in range(64):
        y, core = s // 16, s % 2
        for k in range(3):
            m[k, s * BLK + k] = 1.0
        for i in range(4):
            m[BLK + core * 16 + y * 4 + i, s * BLK + 3 + i] = 1.0
    return jnp.asarray(m, jnp.bfloat16)


def trade(v, axis, mask):
    n = lax.axis_size(axis)
    return lax.ppermute(v, axis, [(i, i ^ mask) for i in range(n)])


SMEM = pl.BlockSpec(memory_space=pltpu.SMEM)
VMEM = pl.BlockSpec(memory_space=pltpu.VMEM)
HBM = pl.BlockSpec(memory_space=pltpu.HBM)


def room(kib):
    return pltpu.CompilerParams(vmem_limit_bytes=kib * 1024)


def call_transform(bins, place, x, total, chunks=4):
    slice_len, rows, _ = x.shape
    n = 2 * bins.shape[0]
    return pl.pallas_call(
        lambda *refs: transform_kernel(total, chunks, *refs),
        out_shape=jax.ShapeDtypeStruct((n, rows, LANES), jnp.float32),
        in_specs=[SMEM, SMEM, HBM],
        out_specs=VMEM,
        scratch_shapes=[pltpu.VMEM(x.shape, jnp.float32), pltpu.SemaphoreType.DMA((chunks,))],
        compiler_params=room(53500),
        name="transform",
    )(bins, place, x)


def call_gram(core, u):
    nb, _, rank, rows, _ = u.shape
    return pl.pallas_call(
        gram_kernel,
        out_shape=[jax.ShapeDtypeStruct((rank // 2, nb * rank), jnp.float32)] * 2,
        in_specs=[SMEM, HBM],
        out_specs=[VMEM] * 2,
        scratch_shapes=[
            pltpu.VMEM((nb, rank, rank), jnp.float32),
            pltpu.VMEM(u.shape, u.dtype),
            pltpu.SemaphoreType.DMA((nb,)),
        ],
        compiler_params=room(52000),
        cost_estimate=pl.CostEstimate(flops=4 * 10**9, bytes_accessed=u.size * 2, transcendentals=0),
        name="gram",
    )(core, u)


def call_project(parts, u, h, n_space):
    nb, _, rank, rows, _ = u.shape
    return pl.pallas_call(
        project_kernel,
        out_shape=(
            jax.ShapeDtypeStruct((nb, 2, rows, LANES), jnp.float32),
            jax.ShapeDtypeStruct((n_space, BLK, LANES), jnp.float32),
        ),
        in_specs=[VMEM, HBM] + [VMEM] * 4,
        out_specs=(VMEM, VMEM),
        scratch_shapes=[
            pltpu.VMEM((3 * LANES * 8, LANES), jnp.float32),
            pltpu.VMEM(u.shape, u.dtype),
            pltpu.SemaphoreType.DMA((nb,)),
        ],
        compiler_params=room(52000),
        cost_estimate=pl.CostEstimate(flops=16 * u.size, bytes_accessed=u.size * 2, transcendentals=0),
        name="project",
    )(parts, u, *h)


def call_update(block_count, g, eigenvalues, spec, u, parts=2):
    nb, _, rank, rows, _ = u.shape
    return pl.pallas_call(
        lambda *refs: update_kernel(parts, *refs),
        out_shape=(
            jax.ShapeDtypeStruct(u.shape, jnp.bfloat16),
            jax.ShapeDtypeStruct((nb, 2, rank, rank), jnp.float32),
        ),
        in_specs=[SMEM] + [VMEM] * 4 + [HBM],
        out_specs=(HBM, VMEM),
        scratch_shapes=[
            pltpu.VMEM((3 * nb * rank, LANES), jnp.float32),
            pltpu.VMEM(u.shape, u.dtype),
            pltpu.VMEM(u.shape, u.dtype),
            pltpu.SemaphoreType.DMA((nb,)),
            pltpu.SemaphoreType.DMA((nb * parts,)),
        ],
        compiler_params=room(52000),
        name="update",
    )(block_count, g, pick_table(rank), eigenvalues, spec, u)


def local(snapshots, bins, eigenvalues, old_basis, block_count):
    slice_len = snapshots.shape[0]
    groups = lax.axis_size("ta")
    total = slice_len * groups
    nb = old_basis.shape[0]
    n_space = lax.axis_size(SPACE)
    place = lax.axis_index("ta").astype(jnp.int32).reshape(1)
    core = lax.axis_index("core").astype(jnp.int32).reshape(1)
    y = lax.axis_index("y")

    terms = call_transform(bins, place, fold(snapshots, 1), total)
    parts = lax.all_to_all(terms, "ta", 0, 0, tiled=True)
    parts = parts.reshape(groups, 2 * nb, *terms.shape[1:])

    u = fold(old_basis, 3)
    u, _ = lax.optimization_barrier((u, terms))
    send, kept = call_gram(core, u)
    h = kept + trade(send, "core", 1)

    n = h.shape[0] // 4
    h = h.reshape(4, n, h.shape[1])
    h = [lax.dynamic_index_in_dim(h, y ^ k, 0, keepdims=False) for k in range(4)]
    h = [h[0]] + [trade(h[k], "y", k) for k in (1, 2, 3)]
    spec, blk = call_project(parts, u, h, n_space)
    g = lax.all_to_all(blk, SPACE, 0, 0, tiled=True).reshape(n_space * BLK, LANES)
    fresh, coherence = call_update(block_count, g, eigenvalues, spec, u)
    return unfold(fresh, 3), coherence


def solution(mesh):
    inner = Mesh(mesh.devices.reshape(4, 4, 8, 2), ("ta",) + SPACE)
    return jax.shard_map(
        local,
        mesh=inner,
        in_specs=(P("ta", None, SPACE), P(), P("ta", None), P("ta", None, None, None, SPACE), P()),
        out_specs=(P("ta", None, None, None, SPACE), P("ta", None, None, None)),
        check_vma=False,
    )
```

```python
import math

import jax
import jax.numpy as jnp
import numpy as np
from jax import lax
from jax.experimental import pallas as pl
from jax.experimental.pallas import tpu as pltpu
from jax.sharding import Mesh, PartitionSpec as P

SPACE = ("y", "z", "core")
LANES = 128
MEETINGS = ((1, 2), (16, 32), (4, 8))
PARTS = 2
UNROLL = 8

UP = ((2, 0), (2, 1), (1, 2), (1, 3))
DOWN = ((2, 2), (2, 3), (3, 0), (3, 1))
KEEP = ((1, 0), (1, 1), (3, 2), (3, 3))
OWN = ((0, 0), (0, 1), (0, 2), (0, 3))
ORDER = UP + DOWN + KEEP + OWN


def fold(v, axis):
    shape = v.shape
    lead, tiles = shape[:-2], shape[-1] // LANES
    v = v.reshape(*lead, 2, tiles, LANES)
    return jnp.swapaxes(v, axis, axis + 1).reshape(*lead, 2 * tiles, LANES)


def unfold(v, axis):
    lead, rows = v.shape[:-2], v.shape[-2]
    v = v.reshape(*lead, rows // 2, 2, LANES)
    return jnp.swapaxes(v, axis, axis + 1).reshape(*lead, 2, rows // 2 * LANES)


def split3(v):
    hi = v.astype(jnp.bfloat16)
    rest = v - hi.astype(jnp.float32)
    mid = rest.astype(jnp.bfloat16)
    low = (rest - mid.astype(jnp.float32)).astype(jnp.bfloat16)
    return hi, mid, low


def transform_kernel(total, chunks, bins_ref, place_ref, x_hbm, *refs):
    *out_refs, x_ref, sems = refs
    slice_len, rows, _ = x_ref.shape
    piece = rows // chunks
    copies = [
        pltpu.make_async_copy(x_hbm.at[:, pl.ds(c * piece, piece)], x_ref.at[:, pl.ds(c * piece, piece)], sems.at[c])
        for c in range(chunks)
    ]
    for copy in copies:
        copy.start()
    n = 2 * len(ORDER)
    place = place_ref[0]
    row = lax.broadcasted_iota(jnp.int32, (n, slice_len), 0)
    t = lax.broadcasted_iota(jnp.int32, (n, slice_len), 1) + place * slice_len
    which = jnp.zeros((n, slice_len), jnp.int32)
    for i, (ahead, b) in enumerate(ORDER):
        which = jnp.where(row // 2 == i, bins_ref[((place + ahead) % 4) * 4 + b], which)
    phase = (which * t + (row % 2) * (total // 4)) % total
    step = 2.0 * math.pi / total
    window = 0.5 - 0.5 * jnp.cos(step * t.astype(jnp.float32))
    table = jnp.cos(step * phase.astype(jnp.float32)) * window * math.sqrt(8.0 / (3.0 * total))
    t_hi = table.astype(jnp.bfloat16)
    t_lo = (table - t_hi.astype(jnp.float32)).astype(jnp.bfloat16)
    left = jnp.concatenate([t_hi, t_lo], axis=0)
    left = jnp.concatenate([left, left], axis=1)
    each = n // len(out_refs)
    for at in range(0, rows, 8):
        if at % piece == 0:
            copies[at // piece].wait()
        x8 = jnp.swapaxes(x_ref[:, at:at + 8, :], 0, 1)
        got = []
        for r in range(0, 8, 2):
            x = jnp.concatenate([x8[r], x8[r + 1]], axis=1)
            hi = x.astype(jnp.bfloat16)
            lo = (x - hi.astype(jnp.float32)).astype(jnp.bfloat16)
            res = jnp.dot(left, jnp.concatenate([hi, lo], axis=0), preferred_element_type=jnp.float32)
            res = res[:n] + res[n:]
            got += [res[:, :LANES], res[:, LANES:]]
        got = jnp.swapaxes(jnp.stack(got, axis=0), 0, 1)
        for i, out_ref in enumerate(out_refs):
            out_ref[:, at:at + 8, :] = got[i * each:(i + 1) * each]


def gram_kernel(u_hbm, h_ref, all_ref, u_ref, sems):
    nb, _, rank, rows, _ = u_ref.shape
    n = 2 * rank

    def load(b):
        return pltpu.make_async_copy(u_hbm.at[b], u_ref.at[b], sems.at[b])

    for b in range(nb):
        load(b).start()

    def one(b, carry):
        load(b).wait()
        vv = jnp.zeros((n, n), jnp.float32)
        for at in range(0, rows, 16):
            u = u_ref[b, :, :, at:at + 16, :].reshape(n, 16, LANES)
            u = jnp.swapaxes(u, 0, 1)
            for r in range(0, 16, 4):
                v = jnp.concatenate([u[r + k] for k in range(4)], axis=1)
                vv = vv + lax.dot_general(v, v, (((1,), (1,)), ((), ())), preferred_element_type=jnp.float32)
        h_re = vv[:rank, :rank] + vv[rank:, rank:]
        h_im = vv[:rank, rank:] - vv[rank:, :rank]
        j = lax.broadcasted_iota(jnp.int32, (rank, rank), 0)
        k = lax.broadcasted_iota(jnp.int32, (rank, rank), 1)
        all_ref[b] = jnp.where(j <= k, h_re, h_im)
        return carry

    lax.fori_loop(0, nb, one, 0)
    h_ref[...] = jnp.concatenate([all_ref[i] for i in range(nb)], axis=1)


def project_kernel(own_ref, a_ref, b_ref, c_ref, d_ref, u_hbm, h_ref, s_ref, all_ref, acc_ref, u_ref, sems):
    nb, _, rank, rows, _ = u_ref.shape
    part = rank // PARTS
    loads = []
    for i in range(nb * PARTS):
        at = pl.ds(i % PARTS * part, part)
        loads.append(pltpu.make_async_copy(u_hbm.at[i // PARTS, :, at], u_ref.at[i // PARTS, :, at], sems.at[i]))
        loads[i].start()
    used = nb * (2 * rank + 1) * 8
    acc_ref[pl.ds(used, acc_ref.shape[0] - used), :] = jnp.zeros((acc_ref.shape[0] - used, LANES), jnp.float32)

    def eight(v):
        return v.reshape(rows // 8, 8, LANES).sum(axis=0)

    for b in range(nb):
        at = 2 * b
        s = []
        for k in (at, at + 1):
            if b < nb // 2:
                s.append(own_ref[k] + b_ref[k + nb] + c_ref[k])
            else:
                s.append(own_ref[k] + a_ref[k] + d_ref[k - nb])
        s_re, s_im = s
        s_ref[b, 0] = s_re
        s_ref[b, 1] = s_im
        acc_ref[pl.ds((2 * nb * rank + b) * 8, 8), :] = eight(s_re * s_re + s_im * s_im)

        def body(j, carry, b=b, s_re=s_re, s_im=s_im):
            u_re = u_ref[b, 0, j].astype(jnp.float32)
            u_im = u_ref[b, 1, j].astype(jnp.float32)
            at = (b * 2 * rank + j) * 8
            acc_ref[pl.ds(pl.multiple_of(at, 8), 8), :] = eight(u_re * s_re + u_im * s_im)
            acc_ref[pl.ds(pl.multiple_of(at + rank * 8, 8), 8), :] = eight(u_re * s_im - u_im * s_re)
            return carry

        for i in range(PARTS):
            loads[b * PARTS + i].wait()
            lax.fori_loop(i * part, (i + 1) * part, body, 0, unroll=UNROLL)

    n = acc_ref.shape[0] // 8
    x = acc_ref[pl.ds(0, n, stride=8), :]
    for k in range(1, 8):
        x = x + acc_ref[pl.ds(k, n, stride=8), :]
    ones = jnp.ones((8, LANES), jnp.bfloat16)
    sums = sum(
        lax.dot_general(ones, v, (((1,), (1,)), ((), ())), preferred_element_type=jnp.float32)
        for v in split3(x)
    )
    rows8 = [sums[0:1, k * LANES:(k + 1) * LANES] for k in range(3)] + [jnp.zeros((5, LANES), jnp.float32)]
    all_ref[...] = jnp.concatenate(rows8 + [h_ref[...]], axis=0)


def update_kernel(parts, count_ref, g_ref, eig_ref, s_ref, u_hbm, out_hbm, coh_ref, coef_ref, u_ref, out_ref, in_sems, sems):
    nb, _, rank, rows, _ = u_ref.shape
    loads = [pltpu.make_async_copy(u_hbm.at[b], u_ref.at[b], in_sems.at[b]) for b in range(nb)]
    for load in loads:
        load.start()

    count = jnp.full((1, 1), count_ref[0], jnp.int32).astype(jnp.float32)
    w_old = count / (count + 1.0)
    w_new = 1.0 / (count + 1.0)
    sums = g_ref[...]
    g = sums[8:]
    j = lax.broadcasted_iota(jnp.int32, (rank, rank), 0)
    k = lax.broadcasted_iota(jnp.int32, (rank, rank), 1)
    eye = j == k

    def col(v):
        return jnp.where(eye, v, 0.0).sum(axis=1, keepdims=True)

    kept = []
    for i in range(nb):
        at = (i % 2) * 2 * rank
        cr = sums[i // 2:i // 2 + 1, at:at + rank]
        ci = sums[i // 2:i // 2 + 1, at + rank:at + 2 * rank]
        power = w_new * sums[2:3, i:i + 1]
        a = w_old * eig_ref[i:i + 1, :]
        cr_c, ci_c, a_c = col(cr), col(ci), col(a)
        diag = a_c * a_c * col(g[:, i * rank:(i + 1) * rank]) + (cr_c * cr_c + ci_c * ci_c) * (w_new * (a_c + a_c + power))
        inv_c = 1.0 / jnp.sqrt(diag + 1e-06)
        for m, v in enumerate((a_c * inv_c, w_new * cr_c * inv_c, w_new * ci_c * inv_c)):
            coef_ref[pl.ds((m * nb + i) * rank, rank), :] = jnp.broadcast_to(v, (rank, LANES))
        kept.append((cr, ci, a, cr_c, ci_c, a_c, inv_c, power))

    block = rank // parts
    copies = []
    for b in range(nb):
        loads[b].wait()
        s_re, s_im = s_ref[b, 0], s_ref[b, 1]

        def body(j, carry, b=b, s_re=s_re, s_im=s_im):
            def coef(m):
                one = coef_ref[pl.ds((m * nb + b) * rank + j, 1), :]
                return jnp.broadcast_to(one, (rows, LANES))

            alpha, beta, gamma = coef(0), coef(1), coef(2)
            u_re = u_ref[b, 0, j].astype(jnp.float32)
            u_im = u_ref[b, 1, j].astype(jnp.float32)
            out_ref[b, 0, j] = (alpha * u_re + (beta * s_re + gamma * s_im)).astype(out_ref.dtype)
            out_ref[b, 1, j] = (alpha * u_im + (beta * s_im - gamma * s_re)).astype(out_ref.dtype)
            return carry

        for part in range(parts):
            lax.fori_loop(part * block, (part + 1) * block, body, 0, unroll=UNROLL)
            at = pl.ds(part * block, block)
            copy = pltpu.make_async_copy(out_ref.at[b, :, at], out_hbm.at[b, :, at], sems.at[b * parts + part])
            copy.start()
            copies.append(copy)

    g_t = g.T
    for i, (cr, ci, a, cr_c, ci_c, a_c, inv_c, power) in enumerate(kept):
        p = g[:, i * rank:(i + 1) * rank]
        p_t = g_t[i * rank:(i + 1) * rank, :]
        h_re = jnp.where(j <= k, p, p_t)
        h_im = jnp.where(j > k, p, jnp.where(eye, 0.0, -p_t))
        both = w_new * (a_c + a + power)
        inv = inv_c * jnp.where(eye, inv_c, 0.0).sum(axis=0, keepdims=True)
        coh_ref[i, 0] = (a_c * a * h_re + (cr_c * cr + ci_c * ci) * both) * inv
        coh_ref[i, 1] = (a_c * a * h_im + (ci_c * cr - cr_c * ci) * both) * inv
    for copy in copies:
        copy.wait()


def meet(v, low, high):
    n = lax.axis_size(SPACE)
    one, two, three = [lax.ppermute(v, SPACE, [(i, i ^ k) for i in range(n)]) for k in (low, high, low | high)]
    return (v + one) + (two + three)


SMEM = pl.BlockSpec(memory_space=pltpu.SMEM)
VMEM = pl.BlockSpec(memory_space=pltpu.VMEM)
HBM = pl.BlockSpec(memory_space=pltpu.HBM)


def room(kib):
    return pltpu.CompilerParams(vmem_limit_bytes=kib * 1024)


def call_transform(bins, place, x, total, chunks=4):
    slice_len, rows, _ = x.shape
    n = 2 * len(ORDER)
    return pl.pallas_call(
        lambda *refs: transform_kernel(total, chunks, *refs),
        out_shape=[jax.ShapeDtypeStruct((n // 4, rows, LANES), jnp.float32)] * 4,
        in_specs=[SMEM, SMEM, HBM],
        out_specs=[VMEM] * 4,
        scratch_shapes=[pltpu.VMEM(x.shape, jnp.float32), pltpu.SemaphoreType.DMA((chunks,))],
        compiler_params=room(53500),
        name="transform",
    )(bins, place, x)


def call_gram(u):
    nb, _, rank, rows, _ = u.shape
    return pl.pallas_call(
        gram_kernel,
        out_shape=jax.ShapeDtypeStruct((rank, nb * rank), jnp.float32),
        in_specs=[HBM],
        out_specs=VMEM,
        scratch_shapes=[
            pltpu.VMEM((nb, rank, rank), jnp.float32),
            pltpu.VMEM(u.shape, u.dtype),
            pltpu.SemaphoreType.DMA((nb,)),
        ],
        compiler_params=room(52000),
        cost_estimate=pl.CostEstimate(flops=4 * 10**9, bytes_accessed=u.size * 2, transcendentals=0),
        name="gram",
    )(u)


def call_project(own, a, b, c, d, u, h):
    nb, _, rank, rows, _ = u.shape
    return pl.pallas_call(
        project_kernel,
        out_shape=(
            jax.ShapeDtypeStruct((nb, 2, rows, LANES), jnp.float32),
            jax.ShapeDtypeStruct((8 + rank, LANES), jnp.float32),
        ),
        in_specs=[VMEM] * 5 + [HBM, VMEM],
        out_specs=(VMEM, VMEM),
        scratch_shapes=[
            pltpu.VMEM((3 * LANES * 8, LANES), jnp.float32),
            pltpu.VMEM(u.shape, u.dtype),
            pltpu.SemaphoreType.DMA((nb * PARTS,)),
        ],
        compiler_params=room(52000),
        cost_estimate=pl.CostEstimate(flops=16 * u.size, bytes_accessed=u.size * 2, transcendentals=0),
        name="project",
    )(own, a, b, c, d, u, h)


def call_update(block_count, g, eigenvalues, spec, u, parts=2):
    nb, _, rank, rows, _ = u.shape
    return pl.pallas_call(
        lambda *refs: update_kernel(parts, *refs),
        out_shape=(
            jax.ShapeDtypeStruct(u.shape, jnp.bfloat16),
            jax.ShapeDtypeStruct((nb, 2, rank, rank), jnp.float32),
        ),
        in_specs=[SMEM] + [VMEM] * 3 + [HBM],
        out_specs=(HBM, VMEM),
        scratch_shapes=[
            pltpu.VMEM((3 * nb * rank, LANES), jnp.float32),
            pltpu.VMEM(u.shape, u.dtype),
            pltpu.VMEM(u.shape, u.dtype),
            pltpu.SemaphoreType.DMA((nb,)),
            pltpu.SemaphoreType.DMA((nb * parts,)),
        ],
        compiler_params=room(52000),
        name="update",
    )(block_count, g, eigenvalues, spec, u)


def local(snapshots, bins, eigenvalues, old_basis, block_count):
    slice_len = snapshots.shape[0]
    groups = lax.axis_size("ta")
    total = slice_len * groups
    nb = old_basis.shape[0]
    place = lax.axis_index("ta").astype(jnp.int32).reshape(1)

    up, down, keep, own = call_transform(bins, place, fold(snapshots, 1), total)
    ring_up = [(i, (i + 1) % groups) for i in range(groups)]
    ring_down = [(i, (i - 1) % groups) for i in range(groups)]
    a = lax.ppermute(up, "ta", ring_up)
    b = lax.ppermute(down, "ta", ring_down)

    u = fold(old_basis, 3)
    u, _ = lax.optimization_barrier((u, up))
    h = call_gram(u)

    c, d = keep[:nb] + a[:nb], keep[nb:] + b[:nb]
    c, d, h = lax.optimization_barrier((c, d, h))
    c = lax.ppermute(c, "ta", ring_up)
    d = lax.ppermute(d, "ta", ring_down)
    spec, g = call_project(own, a, b, c, d, u, h)
    for low, high in MEETINGS:
        g = meet(g, low, high)
    fresh, coherence = call_update(block_count, g, eigenvalues, spec, u)
    return unfold(fresh, 3), coherence


def solution(mesh):
    inner = Mesh(mesh.devices.reshape(4, 4, 8, 2), ("ta",) + SPACE)
    return jax.shard_map(
        local,
        mesh=inner,
        in_specs=(P("ta", None, SPACE), P(), P("ta", None), P("ta", None, None, None, SPACE), P()),
        out_specs=(P("ta", None, None, None, SPACE), P("ta", None, None, None)),
        check_vma=False,
    )
```
